32 devices in a mesh: section: 4 (over y, x), tp: 8 (over z, core).
Axes of the slice: x: 2, y: 2, z: 4, core: 2. Of those that a mesh axis runs over, the one named last changes fastest.
Arguments:
- entering: bfloat16 [2, 3, 32, 4096], P(None, None, None, 'tp'), may hold values from -6 to 6
- output_grad: bfloat16 [2, 3, 32, 4096], P(None, None, None, 'tp'), may hold values from -6 to 6
- live_counts: int32 [2, 3], replicated, may hold values from 1 to 32, as said below
- segment_ids: int32 [2, 3, 32], replicated, may hold values from 0 to 3, never falling along the last dimension, each value on 1 to 16 neighbouring positions
- weight_in: bfloat16 [4, 4096, 11008], P('section', None, 'tp'), may hold values from -0.125 to 0.125
- weight_out: bfloat16 [4, 11008, 4096], P('section', 'tp'), may hold values from -0.078125 to 0.078125
- norm_gain: bfloat16 [4, 4096], P('section'), may hold values from 0.25 to 1.75
- shift_mix: bfloat16 [4, 4096], P('section'), may hold values from 0.099609375 to 0.8984375
Outputs:
- grad_in: bfloat16 [4, 4096, 11008], P('section', None, 'tp')
- grad_out: bfloat16 [4, 11008, 4096], P('section', 'tp')
- grad_gain: float32 [4, 4096], P('section', 'tp')
- grad_mix: float32 [4, 4096], P('section', 'tp')
The draws below stay inside these ranges and needn't reach their ends.
Inputs may be any that keep to these rules, and one draw needn't show every extreme that they name: `live_counts`: in each relay at least one micro-batch has all 32 rows live. `segment_ids`: never falls along the rows of a micro-batch.
All inputs are finite; a program needn't handle non-finite values.
Results may differ from the reference program's by a relative error of at most 0.03.
Values may be sent and summed in bfloat16 or wider, within the bound.
A program may use at most 256 MiB of HBM per device.

```python
import math
import jax
import jax.numpy as jnp
import numpy as np
from jax import lax

D = 4096
FF = 11008
TOK = 32
MB = 3
LAYERS = 4
N_TP = 8


def draw_live_counts(key, part):
    key_counts, key_choice = jax.random.split(key)
    counts = jax.random.randint(key_counts, (2, MB), TOK // 4, TOK + 1)
    chosen = jax.random.randint(key_choice, (2, 1), 0, MB)
    slot_ids = jnp.arange(MB)[None, :]
    return jnp.where(slot_ids == chosen, TOK, counts).astype(jnp.int32)


def spiked(array, key, source, target, parts, factor):
    def block_of(dim):
        return (jnp.arange(array.shape[dim]) // (array.shape[dim] // parts)).reshape((-1,) + (1,) * (array.ndim - 1 - dim))

    first = jax.random.permutation(key, parts)[block_of(target)]
    other_side = (block_of(target) + parts // 2) % parts
    return jnp.where((block_of(source) == first) | (block_of(source) == other_side), factor * array, array)


def block_scale(own_key, extent, cuts, least, largest):
    factor_of = 1.0
    for position, parts in cuts:
        steps = jax.random.uniform(jax.random.fold_in(jax.random.fold_in(own_key, 6), position), (parts,), jnp.float32, least / len(cuts), largest / len(cuts))
        factor_of = factor_of * jnp.repeat(jnp.exp(steps), extent[position] // parts).reshape((-1,) + (1,) * (len(extent) - 1 - position))
    return factor_of


def profile(amount, total, bound, slope):
    portions = [(1 << 20) // math.isqrt(rank ** slope) + 1 for rank in range(2, amount + 1)]
    spare, given = total - bound - (amount - 1), [1] * (amount - 1)
    while spare > 0:
        free = [i for i in range(amount - 1) if given[i] < bound]
        whole, left = sum([portions[i] for i in free]), spare
        for i in free:
            extra = min(bound - given[i], max(1, left * portions[i] // whole), spare)
            given[i] = given[i] + extra
            spare = spare - extra
    return np.array([bound] + given)


def ragged_sizes(own_key, amount, total, limit, skew):
    if amount == 2:
        one = jax.random.randint(own_key, (), max(1, total - limit), min(limit, total - 1) + 1)
        return jnp.stack([one, total - one])
    lengths = jnp.asarray(profile(amount, total, limit, skew), jnp.int32)
    twos = (amount - 1) // 2
    donor, sink = lengths[1:1 + 2 * twos:2], lengths[2:2 + 2 * twos:2]
    room = jnp.minimum(donor - 1, limit - sink)
    moved = jax.random.randint(jax.random.fold_in(own_key, 1), (twos,), 0, 1 << 20) % (room + 1)
    lengths = lengths.at[1:1 + 2 * twos:2].set(donor - moved).at[2:2 + 2 * twos:2].set(sink + moved)
    return lengths[jax.random.permutation(jax.random.fold_in(own_key, 2), amount)]


def normal_values(rng, shape, scale, bound, cuts=(), kind=jnp.bfloat16):
    drawn = jax.random.normal(rng, shape, jnp.float32) * scale
    if len(cuts) > 0:
        drawn = block_scale(rng, shape, cuts, -0.22, 0.18) * drawn
    return jnp.clip(drawn, min=-bound, max=bound).astype(kind)


def noise_with(rng, extent, spread, reach, cuts, heavy, dtype=jnp.bfloat16):
    array = spread * jax.random.normal(rng, extent, jnp.float32)
    if cuts:
        array = array * block_scale(rng, extent, cuts, -0.22, 0.18)
    return jnp.clip(spiked(array, jax.random.fold_in(rng, 3), *heavy), -reach, reach).astype(dtype)


def setup_inputs(seed: int = 0) -> dict:
    streams_of = jax.random.split(jax.random.key(seed), 9)
    entering = normal_values(streams_of[0], (2, MB, TOK, D), 1.0, 6.0, ((3, 8),))
    output_grad = normal_values(streams_of[1], (2, MB, TOK, D), 1.0, 6.0, ((3, 8),))
    live_counts = draw_live_counts(jax.random.fold_in(streams_of[8], 71), 0)
    segment_ids = jax.vmap(lambda own: jnp.searchsorted(jnp.cumsum(ragged_sizes(own, 4, TOK, TOK // 2, 1)), jnp.arange(TOK), side="right"))(jax.random.split(streams_of[3], 2 * MB)).reshape((2, MB, TOK)).astype(jnp.int32)
    weight_in = noise_with(streams_of[4], (LAYERS, D, FF), D ** -0.5, 0.125, ((0, 4), (2, 8)), (2, 1, 8, 2.0))
    weight_out = noise_with(streams_of[5], (LAYERS, FF, D), FF ** -0.5, 0.078125, ((0, 4), (1, 8)), (1, 2, 8, 2.0))
    norm_gain = jnp.clip(1.0 + 0.15 * jax.random.normal(streams_of[6], (LAYERS, D), jnp.float32), 0.25, 1.75).astype(jnp.bfloat16)
    shift_mix = jnp.clip(0.099609375 + 0.7988281 * jax.random.uniform(streams_of[7], (LAYERS, D), jnp.float32) ** block_scale(streams_of[7], (LAYERS, D), ((0, 4),), -0.2, 0.2), 0.099609375, 0.8984375).astype(jnp.bfloat16)
    return {"entering": entering, "output_grad": output_grad, "live_counts": live_counts, "segment_ids": segment_ids, "weight_in": weight_in, "weight_out": weight_out, "norm_gain": norm_gain, "shift_mix": shift_mix}


epsilon = 1e-05

def row_linkage(segment_ids):
    joined = segment_ids[..., 1:] == segment_ids[..., :-1]
    leading = jnp.zeros(segment_ids.shape[:-1] + (1,), jnp.float32)
    return jnp.concatenate([leading, joined.astype(jnp.float32)], axis=-1)

def earlier_rows(values, linkage):
    shifted = jnp.concatenate([jnp.zeros_like(values[..., :1, :]), values[..., :-1, :]], axis=-2)
    return shifted * linkage[..., None]

def later_rows(values, linkage):
    shifted = values[..., 1:, :] * linkage[..., 1:, None]
    return jnp.concatenate([shifted, jnp.zeros_like(values[..., :1, :])], axis=-2)

def silu_slope(pre_act):
    sigmoid = jax.nn.sigmoid(pre_act)
    return sigmoid * (1.0 + pre_act * (1.0 - sigmoid))

def rounded(values):
    return lax.optimization_barrier(values.astype(jnp.bfloat16)).astype(jnp.float32)

def mixed_rows(inputs, linkage, mix_values):
    floats = inputs.astype(jnp.float32)
    earlier = earlier_rows(floats, linkage)
    return (floats, earlier, floats + mix_values * (earlier - floats))

def forward_pieces(inputs, linkage, gain_values, mix_values, first_weights):
    floats, earlier, united = mixed_rows(inputs, linkage, mix_values)
    squares = lax.optimization_barrier(jnp.sum(united * united, axis=-1))
    row_scale = lax.rsqrt(squares / D + epsilon)
    normed = (united * gain_values).astype(jnp.bfloat16)
    summed = jnp.einsum('pmtd,df->pmtf', normed.astype(jnp.float32), first_weights.astype(jnp.float32))
    pre_act = row_scale[..., None] * summed
    hidden = jax.nn.silu(pre_act).astype(jnp.bfloat16)
    return (floats, earlier, united, row_scale, normed, summed, pre_act, hidden)

def reference(entering, output_grad, live_counts, segment_ids, weight_in, weight_out, norm_gain, shift_mix):
    linkage = row_linkage(segment_ids)
    row_index = jnp.arange(TOK)
    live_rows = (row_index[None, None, :] < live_counts[..., None]).astype(jnp.float32)
    hidden_block = FF // N_TP
    layer_inputs = [entering]
    for layer_index in range(LAYERS):
        gain_values = norm_gain[layer_index].astype(jnp.float32)
        mix_values = shift_mix[layer_index].astype(jnp.float32)
        pieces = forward_pieces(layer_inputs[-1], linkage, gain_values, mix_values, weight_in[layer_index])
        floats, hidden = (pieces[0], pieces[7])
        blocks = hidden.astype(jnp.float32).reshape(hidden.shape[:-1] + (N_TP, hidden_block))
        out_weights = weight_out[layer_index].astype(jnp.float32).reshape(N_TP, hidden_block, D)
        partial_value = jnp.einsum('pmtjf,jfd->pmtjd', blocks, out_weights)
        added = lax.optimization_barrier(jnp.sum(rounded(partial_value), axis=3))
        layer_inputs.append((floats + added).astype(jnp.bfloat16))
    upstream = (output_grad.astype(jnp.float32) * live_rows[..., None]).astype(jnp.bfloat16)
    first_list, second_list, gain_list, mix_list = ([], [], [], [])
    for layer_index in reversed(range(LAYERS)):
        gain_values = norm_gain[layer_index].astype(jnp.float32)
        mix_values = shift_mix[layer_index].astype(jnp.float32)
        floats, earlier, united, row_scale, normed, summed, pre_act, hidden = forward_pieces(layer_inputs[layer_index], linkage, gain_values, mix_values, weight_in[layer_index])
        upstream_float = upstream.astype(jnp.float32)
        second_grad = jnp.einsum('pmtf,pmtd->pfd', hidden.astype(jnp.float32), upstream_float)
        grad_hidden = jnp.einsum('pmtd,fd->pmtf', upstream_float, weight_out[layer_index].astype(jnp.float32))
        gate_grad = grad_hidden * silu_slope(pre_act)
        grad_summed = (gate_grad * row_scale[..., None]).astype(jnp.bfloat16)
        grad_rate = lax.optimization_barrier(jnp.sum(gate_grad * summed, axis=-1))
        first_grad = jnp.einsum('pmtd,pmtf->pdf', normed.astype(jnp.float32), grad_summed.astype(jnp.float32))
        blocks = grad_summed.astype(jnp.float32).reshape(grad_summed.shape[:-1] + (N_TP, hidden_block))
        in_weights = weight_in[layer_index].astype(jnp.float32).reshape(D, N_TP, hidden_block)
        partial_value = jnp.einsum('pmtjf,djf->pmtjd', blocks, in_weights)
        grad_normed = lax.optimization_barrier(jnp.sum(rounded(partial_value), axis=3))
        grad_united = grad_normed * gain_values - (grad_rate * row_scale ** 3 / D)[..., None] * united
        gain_grad = lax.optimization_barrier(jnp.sum(grad_normed * united, axis=(1, 2)))
        mix_grad = lax.optimization_barrier(jnp.sum(grad_united * (earlier - floats), axis=(1, 2)))
        below = upstream_float + grad_united * (1.0 - mix_values) + later_rows(grad_united * mix_values, linkage)
        upstream = below.astype(jnp.bfloat16)
        first_list.append((rounded(first_grad[0]) + rounded(first_grad[1])).astype(jnp.bfloat16))
        second_list.append((rounded(second_grad[0]) + rounded(second_grad[1])).astype(jnp.bfloat16))
        gain_list.append(rounded(gain_grad[0]) + rounded(gain_grad[1]))
        mix_list.append(rounded(mix_grad[0]) + rounded(mix_grad[1]))
    grad_in = jnp.stack(first_list[::-1])
    grad_out = jnp.stack(second_list[::-1])
    grad_gain = jnp.stack(gain_list[::-1])
    grad_mix = jnp.stack(mix_list[::-1])
    return (grad_in, grad_out, grad_gain, grad_mix)
```

```python
import functools

import jax
import jax.numpy as jnp
from jax import lax
from jax.experimental import pallas as pl
from jax.experimental.pallas import tpu as pltpu
from jax.sharding import PartitionSpec as P

epsilon = 1e-05
MESH = pl.DeviceIdType.MESH
NT = (((1,), (1,)), ((), ()))
TN = (((0,), (0,)), ((), ()))


def wait_bytes(ref, sem):
    pltpu.make_async_copy(ref, ref, sem).wait()


def relay_kernel(
    n,
    sections,
    live_ref,
    entering_ref,
    upstream_ref,
    segment_ref,
    gain_row,
    mix_row,
    w_in_hbm,
    w_out_hbm,
    normed_ref,
    gate_ref,
    hidden_ref,
    up_ref,
    gain_sums,
    mix_sums,
    ag,
    pair_out,
    pair_in,
    part_out,
    part_in,
    link_ref,
    live_rows,
    gain_ref,
    mix_ref,
    w_in,
    w_out,
    summed_ref,
    hidden_grad,
    scale_ref,
    rate_out,
    rate_in,
    vec_out,
    vec_in,
    ag_send,
    ag_recv,
    pair_send,
    pair_recv,
    rs_send,
    rs_recv,
    rate_send,
    rate_recv,
    vec_send,
    vec_recv,
    w_sem,
):
    me = lax.axis_index("tp")
    sec = lax.axis_index("section")
    packs, tok, width = entering_ref.shape
    micro = packs // 2
    chips = n // 2
    chip = me // 2
    core = lax.rem(me, 2)
    sibling = me + 1 - 2 * core
    last = sections - 1
    bf16, f32 = jnp.bfloat16, jnp.float32

    def chip_at(k):
        value, bit = chip, 1
        while bit <= k:
            if k & bit:
                value = value + bit - 2 * bit * lax.rem(chip // bit, 2)
            bit *= 2
        return value

    away = [chip_at(k) for k in range(chips)]
    near = [2 * c + core for c in away]
    far = [2 * c + 1 - core for c in away]

    barrier = pltpu.get_barrier_semaphore()

    def greet(**device):
        pl.semaphore_signal(barrier, inc=1, device_id=device, device_id_type=MESH)

    for k in range(1, chips):
        greet(tp=near[k])
    greet(tp=sibling)

    @pl.when(sec > 0)
    def _():
        for k in range(chips):
            greet(section=sec - 1, tp=near[k])

    @pl.when(sec < last)
    def _():
        for k in range(chips):
            greet(section=sec + 1, tp=near[k])

    def load_in(j):
        return pltpu.make_async_copy(
            w_in_hbm.at[:, pl.ds(pl.multiple_of(j * width, width), width)],
            w_in.at[j],
            w_sem.at[0, j],
        )

    def load_out(j):
        return pltpu.make_async_copy(
            w_out_hbm.at[:, pl.ds(pl.multiple_of(j * width, width), width)],
            w_out.at[j],
            w_sem.at[1, j],
        )

    for k in range(chips):
        load_in(near[k]).start()
        load_in(far[k]).start()
    for k in range(chips):
        load_out(near[k]).start()
        load_out(far[k]).start()

    square = [lax.broadcasted_iota(jnp.int32, (tok, tok), axis) for axis in range(2)]
    column = lax.broadcasted_iota(jnp.int32, (tok, 1), 0)
    for p in range(2):
        for m in range(micro):
            ids = segment_ref[m, p : p + 1, :].astype(f32)
            here = jnp.sum(jnp.where(square[0] == square[1], ids, 0.0), axis=-1, keepdims=True)
            before = jnp.sum(
                jnp.where(square[0] == square[1] + 1, ids, 0.0), axis=-1, keepdims=True
            )
            joined = jnp.logical_and(here == before, column > 0)
            link_ref[p * micro + m] = jnp.where(joined, 1.0, 0.0)
            live_rows[p * micro + m] = jnp.where(column < live_ref[p, m], 1.0, 0.0)
    for j in range(n):
        own = slice(j * width, (j + 1) * width)
        gain_ref[j] = gain_row[:, own].astype(f32)
        mix_ref[j] = mix_row[:, own].astype(f32)
    vec_out[...] = jnp.zeros_like(vec_out)

    outer = jnp.logical_or(sec == 0, sec == last)

    @pl.when(outer)
    def _():
        pl.semaphore_wait(barrier, 2 * chips)

    @pl.when(jnp.logical_not(outer))
    def _():
        pl.semaphore_wait(barrier, 3 * chips)

    def gather_copy(phase, q, source, peer):
        return pltpu.make_async_remote_copy(
            src_ref=ag.at[phase, q, source],
            dst_ref=ag.at[phase, q, source],
            send_sem=ag_send.at[phase, q],
            recv_sem=ag_recv.at[phase, q, source],
            device_id={"tp": peer},
            device_id_type=MESH,
        )

    def pair_copy(phase, q, target):
        return pltpu.make_async_remote_copy(
            src_ref=pair_out.at[phase, q, target],
            dst_ref=pair_in.at[phase, q, target],
            send_sem=pair_send.at[phase, q],
            recv_sem=pair_recv.at[phase, q, target],
            device_id={"tp": sibling},
            device_id_type=MESH,
        )

    def part_copy(phase, q, target):
        return pltpu.make_async_remote_copy(
            src_ref=part_out.at[phase, q, target],
            dst_ref=part_in.at[phase, q, chip],
            send_sem=rs_send.at[phase, q],
            recv_sem=rs_recv.at[phase, q],
            device_id={"section": sec + 1 - 2 * phase, "tp": 2 * target + core},
            device_id_type=MESH,
        )

    def rate_copy(q):
        return pltpu.make_async_remote_copy(
            src_ref=rate_out.at[q],
            dst_ref=rate_in.at[q],
            send_sem=rate_send.at[q],
            recv_sem=rate_recv.at[q],
            device_id={"tp": sibling},
            device_id_type=MESH,
        )

    def vec_copy(target):
        return pltpu.make_async_remote_copy(
            src_ref=vec_out.at[target],
            dst_ref=vec_in.at[chip],
            send_sem=vec_send,
            recv_sem=vec_recv,
            device_id={"tp": 2 * target + core},
            device_id_type=MESH,
        )

    def rows_of(q):
        return pl.ds(pl.multiple_of(q * tok, tok), tok)

    def spread(phase, q):
        for k in reversed(range(1, chips)):
            gather_copy(phase, q, me, near[k]).start()
        gather_copy(phase, q, me, sibling).start()

    def gathered(phase, q, consume):
        consume(me)
        gather_copy(phase, q, sibling, me).wait_recv()
        consume(sibling)
        for k in range(1, chips):
            gather_copy(phase, q, near[k], me).wait_recv()
            gather_copy(phase, q, near[k], sibling).start()
            consume(near[k])
            if k > 1:
                gather_copy(phase, q, far[k - 1], me).wait_recv()
                consume(far[k - 1])
        if chips > 1:
            gather_copy(phase, q, far[chips - 1], me).wait_recv()
            consume(far[chips - 1])

    def reduced(phase, q):
        wait_bytes(part_in.at[phase, q], rs_recv.at[phase, q])
        total = part_in[phase, q, 0].astype(f32)
        for c in range(1, chips):
            total = total + part_in[phase, q, c].astype(f32)
        return total.astype(bf16)

    def enter_forward(q):
        @pl.when(sec == 0)
        def _():
            ag[0, q, me] = entering_ref[q]

        @pl.when(sec > 0)
        def _():
            ag[0, q, me] = reduced(0, q)

        spread(0, q)

    def enter_backward(q):
        @pl.when(sec == last)
        def _():
            ag[1, q, me] = (upstream_ref[q].astype(f32) * live_rows[q]).astype(bf16)

        @pl.when(sec < last)
        def _():
            ag[1, q, me] = reduced(1, q)

        spread(1, q)

    def scatter(phase, q, values_ref, weights, finish, enter):
        values = values_ref[rows_of(q), :]
        skew = min(2, chips)
        order = list(reversed(range(chips)))
        for i in range(chips + skew):
            if i == skew:
                enter()
            if i < chips:
                k = order[i]
                pair_out[phase, q, away[k]] = jnp.dot(
                    values, weights[far[k]], preferred_element_type=f32
                ).astype(bf16)
                pair_copy(phase, q, away[k]).start()
            if i >= skew:
                k = order[i - skew]
                own = jnp.dot(values, weights[near[k]], preferred_element_type=f32)
                pair_copy(phase, q, away[k]).wait_recv()
                finish(k, own + pair_in[phase, q, away[k]].astype(f32))

    def mixed(q, source):
        floats = ag[0, q, source].astype(f32)
        earlier = pltpu.roll(floats, 1, 0) * link_ref[q]
        delta = earlier - floats
        return floats, delta, floats + mix_ref[source] * delta

    def forward(q):
        sums = []

        def consume(source):
            @pl.when(q == 0)
            def _():
                load_in(source).wait()

            _, _, united = mixed(q, source)
            normed = (united * gain_ref[source]).astype(bf16)
            normed_ref[source, rows_of(q), :] = normed
            dots = lax.dot_general(normed, w_in[source], NT, preferred_element_type=f32)
            squares = jnp.sum(united * united, axis=-1, keepdims=True)
            if sums:
                dots, squares = sums[0] + dots, sums[1] + squares
            sums[:] = [dots, squares]

        gathered(0, q, consume)
        summed, squares = sums
        summed_ref[q] = summed
        row_scale = lax.rsqrt(squares / (n * width) + epsilon)
        scale_ref[q] = jnp.broadcast_to(row_scale, scale_ref.shape[1:])
        pre_act = row_scale * summed
        hidden = (pre_act / (1.0 + jnp.exp(-pre_act))).astype(bf16)
        hidden_ref[rows_of(q), :] = hidden

    def scatter_forward(q):
        @pl.when(q == 0)
        def _():
            for j in range(n):
                load_out(j).wait()

        def finish(k, total):
            if k == 0:
                total = total + ag[0, q, me].astype(f32)
            part_out[0, q, away[k]] = total.astype(bf16)
            part_copy(0, q, away[k]).start()

        def enter():
            @pl.when(q < packs - 1)
            def _():
                enter_forward(q + 1)

        scatter(0, q, hidden_ref, w_out, finish, enter)

    def backward(q):
        sums = []

        def consume(source):
            @pl.when(jnp.logical_and(q == 0, sec == last))
            def _():
                load_out(source).wait()

            values = ag[1, q, source]
            up_ref[source, rows_of(q), :] = values
            dots = lax.dot_general(values, w_out[source], NT, preferred_element_type=f32)
            sums[:] = [sums[0] + dots if sums else dots]

        gathered(1, q, consume)
        hidden_grad[q] = sums[0]

    def scatter_backward(q, enter):
        row_scale = scale_ref[q][:, :1]
        summed = summed_ref[q]
        pre_act = row_scale * summed
        sigmoid = 1.0 / (1.0 + jnp.exp(-pre_act))
        gate_grad = hidden_grad[q] * (sigmoid * (1.0 + pre_act * (1.0 - sigmoid)))
        gate_ref[rows_of(q), :] = (gate_grad * row_scale).astype(bf16)
        rate = jnp.sum(gate_grad * summed, axis=-1, keepdims=True)
        rate_out[q] = jnp.broadcast_to(rate, rate_out.shape[1:])
        rate_copy(q).start()
        relay = q // micro
        factors = []

        def finish(k, total):
            if not factors:
                rate_copy(q).wait_recv()
                both = rate_out[q][:, :1] + rate_in[q][:, :1]
                factors.append(both * (row_scale * row_scale * row_scale) / (n * width))
            target = near[k]
            _, delta, united = mixed(q, target)
            mix = mix_ref[target]
            grad_united = total * gain_ref[target] - factors[0] * united
            later = pltpu.roll(link_ref[q] * (grad_united * mix), tok - 1, 0)
            below = grad_united * (1.0 - mix) + later
            if k == 0:
                below = below + ag[1, q, me].astype(f32)
            part_out[1, q, away[k]] = below.astype(bf16)

            @pl.when(sec > 0)
            def _():
                part_copy(1, q, away[k]).start()

            gain_row_sum = jnp.sum(total * united, axis=0, keepdims=True)
            mix_row_sum = jnp.sum(grad_united * delta, axis=0, keepdims=True)
            vec_out[away[k], relay] += gain_row_sum
            vec_out[away[k], 2 + relay] += mix_row_sum

        scatter(1, q, gate_ref, w_in, finish, enter)

    @pl.when(sec == last)
    def _():
        @pl.loop(0, packs)
        def _(q):
            enter_backward(q)

        @pl.loop(0, packs)
        def _(q):
            backward(q)

    enter_forward(0)

    @pl.loop(0, packs)
    def _(q):
        forward(q)

        @pl.when(sec < last)
        def _():
            scatter_forward(q)

        @pl.when(sec == last)
        def _():
            def enter():
                @pl.when(q < packs - 1)
                def _():
                    enter_forward(q + 1)

            scatter_backward(q, enter)

    @pl.when(sec < last)
    def _():
        enter_backward(0)

        @pl.loop(0, packs)
        def _(q):
            backward(q)

            def enter():
                @pl.when(q < packs - 1)
                def _():
                    enter_backward(q + 1)

            scatter_backward(q, enter)

    for k in range(1, chips):
        vec_copy(away[k]).start()

    @pl.loop(0, packs)
    def _(q):
        def sent(phase):
            wait_bytes(part_out.at[phase, q], rs_send.at[phase, q])

        for phase in range(2):
            wait_bytes(ag.at[phase, q, pl.ds(0, n - 1)], ag_send.at[phase, q])
        wait_bytes(pair_out.at[1, q], pair_send.at[1, q])
        rate_copy(q).wait_send()

        @pl.when(sec < last)
        def _():
            wait_bytes(pair_out.at[0, q], pair_send.at[0, q])
            sent(0)

        @pl.when(sec > 0)
        def _():
            sent(1)

    sums = vec_out[chip]
    if chips > 1:
        wait_bytes(vec_in.at[pl.ds(0, chips - 1)], vec_recv)
        for k in range(1, chips):
            sums = sums + vec_in[away[k]]
        wait_bytes(vec_out.at[pl.ds(0, chips - 1)], vec_send)
    gain_sums[...] = sums[:2]
    mix_sums[...] = sums[2:]


def grads_kernel(
    normed_ref, gate_ref, hidden_ref, up_ref, gain_ref, mix_ref, grad_in, grad_out, gain, mix
):
    def summed(left, right):
        return lax.dot_general(left, right, TN, preferred_element_type=jnp.float32)

    def twice_rounded(acc):
        pair = [acc[p].astype(jnp.bfloat16).astype(jnp.float32) for p in range(2)]
        return pair[0] + pair[1]

    grad_in[0] = summed(gate_ref[...], normed_ref[0]).astype(grad_in.dtype)
    grad_out[0] = summed(hidden_ref[...], up_ref[0]).astype(grad_out.dtype)
    gain[...] = twice_rounded(gain_ref)
    mix[...] = twice_rounded(mix_ref)


def local(
    entering, output_grad, live_counts, segment_ids, weight_in, weight_out, norm_gain, shift_mix
):
    sections = lax.axis_size("section")
    n = lax.axis_size("tp")
    relays, micro, tok, width = entering.shape
    packs = relays * micro
    hidden = weight_in.shape[2]
    width_all = weight_in.shape[1]
    chips = n // 2
    total = packs * tok
    bf16, f32 = jnp.bfloat16, jnp.float32
    vmem = pl.BlockSpec(memory_space=pltpu.VMEM)
    smem = pl.BlockSpec(memory_space=pltpu.SMEM)
    hbm = pl.BlockSpec(memory_space=pl.ANY)
    dma = pltpu.SemaphoreType.DMA
    normed, gate, hidden_rows, up, gain_sums, mix_sums = pl.pallas_call(
        functools.partial(relay_kernel, n, sections),
        out_shape=(
            jax.ShapeDtypeStruct((n, total, width), bf16),
            jax.ShapeDtypeStruct((total, hidden), bf16),
            jax.ShapeDtypeStruct((total, hidden), bf16),
            jax.ShapeDtypeStruct((n, total, width), bf16),
            jax.ShapeDtypeStruct((2, 1, width), f32),
            jax.ShapeDtypeStruct((2, 1, width), f32),
        ),
        in_specs=[smem] + [vmem] * 5 + [hbm] * 2,
        out_specs=(vmem,) * 6,
        scratch_shapes=[
            pltpu.VMEM((2, packs, n, tok, width), bf16),
            pltpu.VMEM((2, packs, chips, tok, width), bf16),
            pltpu.VMEM((2, packs, chips, tok, width), bf16),
            pltpu.VMEM((2, packs, chips, tok, width), bf16),
            pltpu.VMEM((2, packs, chips, tok, width), bf16),
            pltpu.VMEM((packs, tok, 1), f32),
            pltpu.VMEM((packs, tok, 1), f32),
            pltpu.VMEM((n, 1, width), f32),
            pltpu.VMEM((n, 1, width), f32),
            pltpu.VMEM((n, hidden, width), bf16),
            pltpu.VMEM((n, hidden, width), bf16),
            pltpu.VMEM((packs, tok, hidden), f32),
            pltpu.VMEM((packs, tok, hidden), f32),
            pltpu.VMEM((packs, tok, 128), f32),
            pltpu.VMEM((packs, tok, 128), f32),
            pltpu.VMEM((packs, tok, 128), f32),
            pltpu.VMEM((chips, 4, 1, width), f32),
            pltpu.VMEM((chips, 4, 1, width), f32),
            dma((2, packs)),
            dma((2, packs, n)),
            dma((2, packs)),
            dma((2, packs, chips)),
            dma((2, packs)),
            dma((2, packs)),
            dma((packs,)),
            dma((packs,)),
            dma,
            dma,
            dma((2, n)),
        ],
        compiler_params=pltpu.CompilerParams(
            collective_id=0, has_side_effects=True, vmem_limit_bytes=60 * 1024 * 1024
        ),
        name="relays",
    )(
        live_counts,
        entering.reshape(packs, tok, width),
        output_grad.reshape(packs, tok, width),
        jnp.swapaxes(segment_ids, 0, 1),
        norm_gain,
        shift_mix,
        jnp.swapaxes(weight_in[0], 0, 1),
        weight_out[0],
    )

    part = pl.BlockSpec((1, total, width), lambda j: (j, 0, 0))
    whole = pl.BlockSpec((total, hidden), lambda j: (0, 0))
    sums = pl.BlockSpec((2, 1, width), lambda j: (0, 0, 0))
    row = pl.BlockSpec((1, width), lambda j: (0, 0))
    grad_in, grad_out, gain, mix = pl.pallas_call(
        grads_kernel,
        grid=(n,),
        out_shape=(
            jax.ShapeDtypeStruct((1, hidden, width_all), bf16),
            jax.ShapeDtypeStruct((1, hidden, width_all), bf16),
            jax.ShapeDtypeStruct((1, width), f32),
            jax.ShapeDtypeStruct((1, width), f32),
        ),
        in_specs=[part, whole, whole, part, sums, sums],
        out_specs=(
            pl.BlockSpec((1, hidden, width), lambda j: (0, 0, j)),
            pl.BlockSpec((1, hidden, width), lambda j: (0, 0, j)),
            row,
            row,
        ),
        compiler_params=pltpu.CompilerParams(
            dimension_semantics=("arbitrary",), vmem_limit_bytes=60 * 1024 * 1024
        ),
        name="weight_grads",
    )(normed, gate, hidden_rows, up, gain_sums, mix_sums)
    return jnp.swapaxes(grad_in, 1, 2), grad_out, gain, mix


def solution(mesh):
    in_specs = (
        P(None, None, None, "tp"),
        P(None, None, None, "tp"),
        P(),
        P(),
        P("section", None, "tp"),
        P("section", "tp", None),
        P("section", None),
        P("section", None),
    )
    out_specs = (
        P("section", None, "tp"),
        P("section", "tp", None),
        P("section", "tp"),
        P("section", "tp"),
    )
    return jax.shard_map(local, mesh=mesh, in_specs=in_specs, out_specs=out_specs, check_vma=False)
```

```python
import functools

import jax
import jax.numpy as jnp
from jax import lax
from jax.experimental import pallas as pl
from jax.experimental.pallas import tpu as pltpu
from jax.sharding import PartitionSpec as P

epsilon = 1e-05
MESH = pl.DeviceIdType.MESH
NT = (((1,), (1,)), ((), ()))
TN = (((0,), (0,)), ((), ()))
FORWARD = ((6, 1),)
BACKWARD = ((6, 1),)


def wait_bytes(ref, sem):
    pltpu.make_async_copy(ref, ref, sem).wait()


def relay_kernel(
    n,
    sections,
    plans,
    live_ref,
    entering_ref,
    upstream_ref,
    segment_ref,
    gain_row,
    mix_row,
    w_in_hbm,
    w_out_hbm,
    normed_ref,
    gate_ref,
    hidden_ref,
    up_ref,
    gain_sums,
    mix_sums,
    ag,
    pair_out,
    pair_in,
    part_out,
    part_in,
    link_ref,
    live_rows,
    gain_ref,
    mix_ref,
    w_in,
    w_out,
    summed_ref,
    hidden_grad,
    scale_ref,
    rate_out,
    rate_in,
    vec_out,
    vec_in,
    ag_send,
    ag_recv,
    pair_send,
    pair_recv,
    rs_send,
    rs_recv,
    rate_send,
    rate_recv,
    vec_send,
    vec_recv,
    w_sem,
):
    me = lax.axis_index("tp")
    sec = lax.axis_index("section")
    _, micro, tok, width = entering_ref.shape
    packs = 2 * micro
    chips = n // 2
    chip = me // 2
    core = lax.rem(me, 2)
    sibling = me + 1 - 2 * core
    last = sections - 1
    bf16, f32 = jnp.bfloat16, jnp.float32

    def chip_at(k):
        value, bit = chip, 1
        while bit <= k:
            if k & bit:
                value = value + bit - 2 * bit * lax.rem(chip // bit, 2)
            bit *= 2
        return value

    away = [chip_at(k) for k in range(chips)]
    span = min(2, chips)
    near = [2 * c + core for c in away]
    far = [2 * c + 1 - core for c in away]

    barrier = pltpu.get_barrier_semaphore()

    def greet(**device):
        pl.semaphore_signal(barrier, inc=1, device_id=device, device_id_type=MESH)

    for k in range(1, chips):
        greet(tp=near[k])
    greet(tp=sibling)

    @pl.when(sec > 0)
    def _():
        for k in range(chips):
            greet(section=sec - 1, tp=near[k])

    @pl.when(sec < last)
    def _():
        for k in range(chips):
            greet(section=sec + 1, tp=near[k])

    def load_in(j):
        return pltpu.make_async_copy(
            w_in_hbm.at[:, pl.ds(pl.multiple_of(j * width, width), width)],
            w_in.at[j],
            w_sem.at[0, j],
        )

    def load_out(j):
        return pltpu.make_async_copy(
            w_out_hbm.at[:, pl.ds(pl.multiple_of(j * width, width), width)],
            w_out.at[j],
            w_sem.at[1, j],
        )

    @pl.when(sec == last)
    def _():
        for j in range(n):
            load_out(j).start()

    for j in range(n):
        load_in(j).start()

    square = [lax.broadcasted_iota(jnp.int32, (tok, tok), axis) for axis in range(2)]
    column = lax.broadcasted_iota(jnp.int32, (tok, 1), 0)
    for p in range(2):
        for m in range(micro):
            ids = segment_ref[m, p : p + 1, :].astype(f32)
            here = jnp.sum(jnp.where(square[0] == square[1], ids, 0.0), axis=-1, keepdims=True)
            before = jnp.sum(
                jnp.where(square[0] == square[1] + 1, ids, 0.0), axis=-1, keepdims=True
            )
            joined = jnp.logical_and(here == before, column > 0)
            link_ref[2 * m + p] = jnp.where(joined, 1.0, 0.0)
            live_rows[2 * m + p] = jnp.where(column < live_ref[p, m], 1.0, 0.0)
    for j in range(n):
        own = slice(j * width, (j + 1) * width)
        gain_ref[j] = gain_row[:, own].astype(f32)
        mix_ref[j] = mix_row[:, own].astype(f32)
    vec_out[...] = jnp.zeros_like(vec_out)

    outer = jnp.logical_or(sec == 0, sec == last)

    @pl.when(outer)
    def _():
        pl.semaphore_wait(barrier, 2 * chips)

    @pl.when(jnp.logical_not(outer))
    def _():
        pl.semaphore_wait(barrier, 3 * chips)

    def gather_copy(phase, q, w, source, peer):
        return pltpu.make_async_remote_copy(
            src_ref=ag.at[phase, pl.ds(q, w), source],
            dst_ref=ag.at[phase, pl.ds(q, w), source],
            send_sem=ag_send.at[phase],
            recv_sem=ag_recv.at[phase, q, source],
            device_id={"tp": peer},
            device_id_type=MESH,
        )

    def pair_copy(phase, q, w, target):
        first = target - lax.rem(target, span)
        return pltpu.make_async_remote_copy(
            src_ref=pair_out.at[phase, pl.ds(q, w), pl.ds(first, span)],
            dst_ref=pair_in.at[phase, pl.ds(q, w), pl.ds(first, span)],
            send_sem=pair_send.at[phase],
            recv_sem=pair_recv.at[phase, q, first],
            device_id={"tp": sibling},
            device_id_type=MESH,
        )

    def part_copy(phase, q, target):
        return pltpu.make_async_remote_copy(
            src_ref=part_out.at[phase, q, target],
            dst_ref=part_in.at[phase, q, chip],
            send_sem=rs_send.at[phase],
            recv_sem=rs_recv.at[phase, q],
            device_id={"section": sec + 1 - 2 * phase, "tp": 2 * target + core},
            device_id_type=MESH,
        )

    def rate_copy(q, w):
        return pltpu.make_async_remote_copy(
            src_ref=rate_out.at[pl.ds(q, w)],
            dst_ref=rate_in.at[pl.ds(q, w)],
            send_sem=rate_send,
            recv_sem=rate_recv.at[q],
            device_id={"tp": sibling},
            device_id_type=MESH,
        )

    def vec_copy(target):
        return pltpu.make_async_remote_copy(
            src_ref=vec_out.at[target],
            dst_ref=vec_in.at[chip],
            send_sem=vec_send,
            recv_sem=vec_recv,
            device_id={"tp": 2 * target + core},
            device_id_type=MESH,
        )

    def rows_of(q, w):
        return pl.ds(pl.multiple_of(q * tok, tok), w * tok)

    def stacked(ref, q, w, *rest):
        if rest:
            value = ref[pl.ds(q, w), rest[0]]
        else:
            value = ref[pl.ds(q, w)]
        return value.reshape((w * tok, value.shape[-1]))

    def spread(phase, q, w):
        for k in reversed(range(1, chips)):
            gather_copy(phase, q, w, me, near[k]).start()
        gather_copy(phase, q, w, me, sibling).start()

    def gathered(phase, q, w, consume, enter):
        gather_copy(phase, q, w, sibling, me).wait_recv()
        consume([me, sibling])
        ready = []
        for k in range(1, chips):
            gather_copy(phase, q, w, near[k], me).wait_recv()
            gather_copy(phase, q, w, near[k], sibling).start()
            ready.append(near[k])
            if k > 2:
                gather_copy(phase, q, w, far[k - 2], me).wait_recv()
                ready.append(far[k - 2])
            if k > 1:
                consume(ready)
                ready = []
        enter()
        for k in range(max(1, chips - 2), chips):
            gather_copy(phase, q, w, far[k], me).wait_recv()
            ready.append(far[k])
        if ready:
            consume(ready)

    def reduced(phase, q):
        wait_bytes(part_in.at[phase, q], rs_recv.at[phase, q])
        total = part_in[phase, q, 0].astype(f32)
        for c in range(1, chips):
            total = total + part_in[phase, q, c].astype(f32)
        return total.astype(bf16)

    def enter_forward(q, w):
        @pl.when(sec == 0)
        def _():
            for j in range(w):
                ag[0, q + j, me] = entering_ref[lax.rem(q + j, 2), (q + j) // 2]

        @pl.when(sec > 0)
        def _():
            for j in range(w):
                ag[0, q + j, me] = reduced(0, q + j)

        spread(0, q, w)

    def enter_backward(q, w):
        @pl.when(sec == last)
        def _():
            for j in range(w):
                values = upstream_ref[lax.rem(q + j, 2), (q + j) // 2].astype(f32)
                ag[1, q + j, me] = (values * live_rows[q + j]).astype(bf16)

        @pl.when(sec < last)
        def _():
            for j in range(w):
                ag[1, q + j, me] = reduced(1, q + j)

        spread(1, q, w)

    def scatter(phase, q, w, values_ref, weights, convert, send):
        values = values_ref[rows_of(q, w), :]
        order = list(reversed(range(chips)))
        groups = [order[i : i + span] for i in range(0, chips, span)]

        def product(j):
            return jnp.dot(values, weights[j], preferred_element_type=f32)

        def combine(group, owns):
            pair_copy(phase, q, w, away[group[0]]).wait_recv()
            return [
                own + stacked(pair_in.at[phase], q, w, away[k]).astype(f32)
                for k, own in zip(group, owns)
            ]

        for group in groups:
            for k in group:
                value = product(far[k]).astype(bf16)
                pair_out[phase, pl.ds(q, w), away[k]] = value.reshape((w, tok, width))
            pair_copy(phase, q, w, away[group[0]]).start()
        ahead_owns = [product(near[k]) for k in groups[0]]
        for i, group in enumerate(groups):
            totals = combine(group, ahead_owns)
            if i + 1 < len(groups):
                ahead_owns = [product(near[k]) for k in groups[i + 1]]
            for k, total in zip(group, totals):
                value = convert(k, total).astype(bf16)
                part_out[phase, pl.ds(q, w), away[k]] = value.reshape((w, tok, width))
            send(group)

    def mixed(q, w, source):
        floats = stacked(ag.at[0], q, w, source).astype(f32)
        earlier = pltpu.roll(floats, 1, 0) * stacked(link_ref, q, w)
        delta = earlier - floats
        return floats, delta, floats + mix_ref[source] * delta

    def forward(q, w, enter):
        sums = []

        @pl.when(q == 0)
        def _():
            for j in range(n):
                load_in(j).wait()

            @pl.when(sec < last)
            def _():
                for j in range(n):
                    load_out(j).start()

        def consume(sources):
            for source in sources:
                _, _, united = mixed(q, w, source)
                normed = (united * gain_ref[source]).astype(bf16)
                normed_ref[source, rows_of(q, w), :] = normed
                dots = lax.dot_general(normed, w_in[source], NT, preferred_element_type=f32)
                squares = united * united
                squares = sum(squares[:, c : c + 128] for c in range(0, width, 128))
                if sums:
                    dots, squares = sums[0] + dots, sums[1] + squares
                sums[:] = [dots, squares]

        gathered(0, q, w, consume, enter)
        summed, squares = sums
        summed_ref[rows_of(q, w), :] = summed
        squares = jnp.sum(squares, axis=-1, keepdims=True)
        row_scale = lax.rsqrt(squares / (n * width) + epsilon)
        scale_ref[rows_of(q, w), :] = jnp.broadcast_to(row_scale, (w * tok, 128))
        pre_act = row_scale * summed
        hidden = (pre_act / (1.0 + jnp.exp(-pre_act))).astype(bf16)
        hidden_ref[rows_of(q, w), :] = hidden

    def scatter_forward(q, w):
        @pl.when(q == 0)
        def _():
            for j in range(n):
                load_out(j).wait()

        def convert(k, total):
            return total + stacked(ag.at[0], q, w, me).astype(f32) if k == 0 else total

        def send(group):
            for j in range(w):
                for k in group:
                    part_copy(0, q + j, away[k]).start()

        scatter(0, q, w, hidden_ref, w_out, convert, send)

    def backward(q, w, enter):
        sums = []

        def consume(sources):
            for source in sources:
                values = stacked(ag.at[1], q, w, source)
                up_ref[source, rows_of(q, w), :] = values
                dots = lax.dot_general(values, w_out[source], NT, preferred_element_type=f32)
                sums[:] = [sums[0] + dots if sums else dots]

        gathered(1, q, w, consume, enter)
        hidden_grad[rows_of(q, w), :] = sums[0]

    def scatter_backward(q, w):
        row_scale = scale_ref[rows_of(q, w), :][:, :1]
        summed = summed_ref[rows_of(q, w), :]
        pre_act = row_scale * summed
        sigmoid = 1.0 / (1.0 + jnp.exp(-pre_act))
        gate_grad = hidden_grad[rows_of(q, w), :] * (sigmoid * (1.0 + pre_act * (1.0 - sigmoid)))
        gate_ref[rows_of(q, w), :] = (gate_grad * row_scale).astype(bf16)
        rate = jnp.sum(gate_grad * summed, axis=-1, keepdims=True)
        rate_out[pl.ds(q, w)] = jnp.broadcast_to(rate, (w * tok, 128)).reshape((w, tok, 128))
        rate_copy(q, w).start()
        factors = []

        def convert(k, total):
            if not factors:
                rate_copy(q, w).wait_recv()
                both = stacked(rate_out, q, w)[:, :1] + stacked(rate_in, q, w)[:, :1]
                factors.append(both * (row_scale * row_scale * row_scale) / (n * width))
            target = near[k]
            _, delta, united = mixed(q, w, target)
            mix = mix_ref[target]
            grad_united = total * gain_ref[target] - factors[0] * united
            moved = stacked(link_ref, q, w) * (grad_united * mix)
            below = grad_united * (1.0 - mix) + pltpu.roll(moved, w * tok - 1, 0)
            if k == 0:
                below = below + stacked(ag.at[1], q, w, me).astype(f32)
            gain_rows, mix_rows = total * united, grad_united * delta
            for j in range(w):
                own = slice(j * tok, (j + 1) * tok)
                p = lax.rem(q + j, 2)
                vec_out[away[k], p] += jnp.sum(gain_rows[own], axis=0, keepdims=True)
                vec_out[away[k], 2 + p] += jnp.sum(mix_rows[own], axis=0, keepdims=True)
            return below

        def send(group):
            @pl.when(sec > 0)
            def _():
                for j in range(w):
                    for k in group:
                        part_copy(1, q + j, away[k]).start()

        scatter(1, q, w, gate_ref, w_in, convert, send)

    def runs(plan, enter, work):
        starts = [sum(c * w for c, w in plan[:i]) for i in range(len(plan))]
        for i, (count, w) in enumerate(plan):

            @pl.loop(0, count)
            def _(g, i=i, count=count, w=w):
                q = starts[i] + g * w

                def step():
                    if count > 1:

                        @pl.when(g < count - 1)
                        def _():
                            enter(q + w, w)

                    if i + 1 < len(plan):

                        @pl.when(g == count - 1)
                        def _():
                            enter(starts[i + 1], plan[i + 1][1])

                work(q, w, step)

    @pl.when(sec == last)
    def _():
        @pl.loop(0, packs)
        def _(q):
            enter_backward(q, 1)

        for j in range(n):
            load_out(j).wait()

        @pl.loop(0, packs)
        def _(q):
            backward(q, 1, lambda: None)

    def work_forward(q, w, step):
        forward(q, w, step)

        @pl.when(sec < last)
        def _():
            scatter_forward(q, w)

        @pl.when(sec == last)
        def _():
            scatter_backward(q, w)

    def work_backward(q, w, step):
        backward(q, w, step)
        scatter_backward(q, w)

    enter_forward(0, plans[0][0][1])
    runs(plans[0], enter_forward, work_forward)

    @pl.when(sec < last)
    def _():
        enter_backward(0, plans[1][0][1])
        runs(plans[1], enter_backward, work_backward)

    for k in range(1, chips):
        vec_copy(away[k]).start()
    for phase in range(2):
        wait_bytes(ag.at[phase, :, pl.ds(0, n - 1)], ag_send.at[phase])
    wait_bytes(pair_out.at[1], pair_send.at[1])
    wait_bytes(rate_out, rate_send)

    @pl.when(sec < last)
    def _():
        wait_bytes(pair_out.at[0], pair_send.at[0])
        wait_bytes(part_out.at[0], rs_send.at[0])

    @pl.when(sec > 0)
    def _():
        wait_bytes(part_out.at[1], rs_send.at[1])

    sums = vec_out[chip]
    if chips > 1:
        wait_bytes(vec_in.at[pl.ds(0, chips - 1)], vec_recv)
        for k in range(1, chips):
            sums = sums + vec_in[away[k]]
        wait_bytes(vec_out.at[pl.ds(0, chips - 1)], vec_send)
    gain_sums[...] = sums[:2]
    mix_sums[...] = sums[2:]


def grads_kernel(
    normed_ref, gate_ref, hidden_ref, up_ref, gain_ref, mix_ref, grad_in, grad_out, gain, mix
):
    def summed(left, right):
        return lax.dot_general(left, right, TN, preferred_element_type=jnp.float32)

    def twice_rounded(acc):
        pair = [acc[p].astype(jnp.bfloat16).astype(jnp.float32) for p in range(2)]
        return pair[0] + pair[1]

    grad_in[0] = summed(gate_ref[...], normed_ref[0]).astype(grad_in.dtype)
    grad_out[0] = summed(hidden_ref[...], up_ref[0]).astype(grad_out.dtype)
    gain[...] = twice_rounded(gain_ref)
    mix[...] = twice_rounded(mix_ref)


def local(
    entering, output_grad, live_counts, segment_ids, weight_in, weight_out, norm_gain, shift_mix
):
    sections = lax.axis_size("section")
    n = lax.axis_size("tp")
    relays, micro, tok, width = entering.shape
    packs = relays * micro
    plans = (FORWARD, BACKWARD)
    hidden = weight_in.shape[2]
    width_all = weight_in.shape[1]
    chips = n // 2
    total = packs * tok
    bf16, f32 = jnp.bfloat16, jnp.float32
    vmem = pl.BlockSpec(memory_space=pltpu.VMEM)
    smem = pl.BlockSpec(memory_space=pltpu.SMEM)
    hbm = pl.BlockSpec(memory_space=pl.ANY)
    dma = pltpu.SemaphoreType.DMA
    normed, gate, hidden_rows, up, gain_sums, mix_sums = pl.pallas_call(
        functools.partial(relay_kernel, n, sections, plans),
        out_shape=(
            jax.ShapeDtypeStruct((n, total, width), bf16),
            jax.ShapeDtypeStruct((total, hidden), bf16),
            jax.ShapeDtypeStruct((total, hidden), bf16),
            jax.ShapeDtypeStruct((n, total, width), bf16),
            jax.ShapeDtypeStruct((2, 1, width), f32),
            jax.ShapeDtypeStruct((2, 1, width), f32),
        ),
        in_specs=[smem] + [vmem] * 5 + [hbm] * 2,
        out_specs=(vmem,) * 6,
        scratch_shapes=[
            pltpu.VMEM((2, packs, n, tok, width), bf16),
            pltpu.VMEM((2, packs, chips, tok, width), bf16),
            pltpu.VMEM((2, packs, chips, tok, width), bf16),
            pltpu.VMEM((2, packs, chips, tok, width), bf16),
            pltpu.VMEM((2, packs, chips, tok, width), bf16),
            pltpu.VMEM((packs, tok, 1), f32),
            pltpu.VMEM((packs, tok, 1), f32),
            pltpu.VMEM((n, 1, width), f32),
            pltpu.VMEM((n, 1, width), f32),
            pltpu.VMEM((n, hidden, width), bf16),
            pltpu.VMEM((n, hidden, width), bf16),
            pltpu.VMEM((total, hidden), f32),
            pltpu.VMEM((total, hidden), f32),
            pltpu.VMEM((total, 128), f32),
            pltpu.VMEM((packs, tok, 128), f32),
            pltpu.VMEM((packs, tok, 128), f32),
            pltpu.VMEM((chips, 4, 1, width), f32),
            pltpu.VMEM((chips, 4, 1, width), f32),
            dma((2,)),
            dma((2, packs, n)),
            dma((2,)),
            dma((2, packs, chips)),
            dma((2,)),
            dma((2, packs)),
            dma,
            dma((packs,)),
            dma,
            dma,
            dma((2, n)),
        ],
        compiler_params=pltpu.CompilerParams(
            collective_id=0, has_side_effects=True, vmem_limit_bytes=60 * 1024 * 1024
        ),
        name="relays",
    )(
        live_counts,
        entering,
        output_grad,
        jnp.swapaxes(segment_ids, 0, 1),
        norm_gain,
        shift_mix,
        jnp.swapaxes(weight_in[0], 0, 1),
        weight_out[0],
    )

    part = pl.BlockSpec((1, total, width), lambda j: (j, 0, 0))
    whole = pl.BlockSpec((total, hidden), lambda j: (0, 0))
    sums = pl.BlockSpec((2, 1, width), lambda j: (0, 0, 0))
    row = pl.BlockSpec((1, width), lambda j: (0, 0))
    grad_in, grad_out, gain, mix = pl.pallas_call(
        grads_kernel,
        grid=(n,),
        out_shape=(
            jax.ShapeDtypeStruct((1, hidden, width_all), bf16),
            jax.ShapeDtypeStruct((1, hidden, width_all), bf16),
            jax.ShapeDtypeStruct((1, width), f32),
            jax.ShapeDtypeStruct((1, width), f32),
        ),
        in_specs=[part, whole, whole, part, sums, sums],
        out_specs=(
            pl.BlockSpec((1, hidden, width), lambda j: (0, 0, j)),
            pl.BlockSpec((1, hidden, width), lambda j: (0, 0, j)),
            row,
            row,
        ),
        compiler_params=pltpu.CompilerParams(
            dimension_semantics=("arbitrary",), vmem_limit_bytes=60 * 1024 * 1024
        ),
        name="weight_grads",
    )(normed, gate, hidden_rows, up, gain_sums, mix_sums)
    return jnp.swapaxes(grad_in, 1, 2), grad_out, gain, mix


def solution(mesh):
    in_specs = (
        P(None, None, None, "tp"),
        P(None, None, None, "tp"),
        P(),
        P(),
        P("section", None, "tp"),
        P("section", "tp", None),
        P("section", None),
        P("section", None),
    )
    out_specs = (
        P("section", None, "tp"),
        P("section", "tp", None),
        P("section", "tp"),
        P("section", "tp"),
    )
    return jax.shard_map(local, mesh=mesh, in_specs=in_specs, out_specs=out_specs, check_vma=False)
```

```python
import functools

import jax
import jax.numpy as jnp
from jax import lax
from jax.experimental import pallas as pl
from jax.experimental.pallas import tpu as pltpu
from jax.sharding import PartitionSpec as P

epsilon = 1e-05
MESH = pl.DeviceIdType.MESH
NT = (((1,), (1,)), ((), ()))
TN = (((0,), (0,)), ((), ()))
FORWARD = ((6, 1),)
BACKWARD = ((6, 1),)


def wait_bytes(ref, sem):
    pltpu.make_async_copy(ref, ref, sem).wait()


def relay_kernel(
    n,
    sections,
    plans,
    live_ref,
    entering_ref,
    upstream_ref,
    segment_ref,
    gain_row,
    mix_row,
    w_in_hbm,
    w_out_hbm,
    wide_ref,
    deep_ref,
    vec_sums,
    ag,
    pair_out,
    pair_in,
    part_out,
    part_in,
    link_ref,
    live_rows,
    gain_ref,
    mix_ref,
    w_in,
    w_out,
    summed_ref,
    hidden_grad,
    scale_ref,
    rate_out,
    rate_in,
    vec_out,
    vec_in,
    ag_send,
    ag_recv,
    pair_send,
    pair_recv,
    rs_send,
    rs_recv,
    rate_send,
    rate_recv,
    vec_send,
    vec_recv,
    w_sem,
):
    me = lax.axis_index("tp")
    sec = lax.axis_index("section")
    _, micro, tok, width = entering_ref.shape
    packs = 2 * micro
    normed_ref, up_ref = wide_ref.at[0], wide_ref.at[1]
    gate_ref, hidden_ref = deep_ref.at[0], deep_ref.at[1]
    chips = n // 2
    chip = me // 2
    core = lax.rem(me, 2)
    sibling = me + 1 - 2 * core
    last = sections - 1
    bf16, f32 = jnp.bfloat16, jnp.float32

    def chip_at(k):
        value, bit = chip, 1
        while bit <= k:
            if k & bit:
                value = value + bit - 2 * bit * lax.rem(chip // bit, 2)
            bit *= 2
        return value

    away = [chip_at(k) for k in range(chips)]
    span = min(2, chips)
    near = [2 * c + core for c in away]
    far = [2 * c + 1 - core for c in away]

    barrier = pltpu.get_barrier_semaphore()

    def greet(**device):
        pl.semaphore_signal(barrier, inc=1, device_id=device, device_id_type=MESH)

    for k in range(1, chips):
        greet(tp=near[k])
    greet(tp=sibling)

    @pl.when(sec > 0)
    def _():
        for k in range(chips):
            greet(section=sec - 1, tp=near[k])

    @pl.when(sec < last)
    def _():
        for k in range(chips):
            greet(section=sec + 1, tp=near[k])

    def load_in(j):
        return pltpu.make_async_copy(
            w_in_hbm.at[:, pl.ds(pl.multiple_of(j * width, width), width)],
            w_in.at[j],
            w_sem.at[0, j],
        )

    def load_out(j):
        return pltpu.make_async_copy(
            w_out_hbm.at[:, pl.ds(pl.multiple_of(j * width, width), width)],
            w_out.at[j],
            w_sem.at[1, j],
        )

    @pl.when(sec == last)
    def _():
        for j in range(n):
            load_out(j).start()

    for j in range(n):
        load_in(j).start()

    square = [lax.broadcasted_iota(jnp.int32, (tok, tok), axis) for axis in range(2)]
    column = lax.broadcasted_iota(jnp.int32, (tok, 1), 0)
    for p in range(2):
        for m in range(micro):
            ids = segment_ref[m, p : p + 1, :].astype(f32)
            here = jnp.sum(jnp.where(square[0] == square[1], ids, 0.0), axis=-1, keepdims=True)
            before = jnp.sum(
                jnp.where(square[0] == square[1] + 1, ids, 0.0), axis=-1, keepdims=True
            )
            joined = jnp.logical_and(here == before, column > 0)
            link_ref[2 * m + p] = jnp.where(joined, 1.0, 0.0)
            live_rows[2 * m + p] = jnp.where(column < live_ref[p, m], 1.0, 0.0)
    for j in range(n):
        own = slice(j * width, (j + 1) * width)
        gain_ref[j] = gain_row[:, own].astype(f32)
        mix_ref[j] = mix_row[:, own].astype(f32)
    vec_out[...] = jnp.zeros_like(vec_out)

    outer = jnp.logical_or(sec == 0, sec == last)

    @pl.when(outer)
    def _():
        pl.semaphore_wait(barrier, 2 * chips)

    @pl.when(jnp.logical_not(outer))
    def _():
        pl.semaphore_wait(barrier, 3 * chips)

    def gather_copy(phase, q, w, source, peer):
        return pltpu.make_async_remote_copy(
            src_ref=ag.at[phase, pl.ds(q, w), source],
            dst_ref=ag.at[phase, pl.ds(q, w), source],
            send_sem=ag_send.at[phase],
            recv_sem=ag_recv.at[phase, q, source],
            device_id={"tp": peer},
            device_id_type=MESH,
        )

    def pair_copy(phase, q, w, target):
        first = target - lax.rem(target, span)
        return pltpu.make_async_remote_copy(
            src_ref=pair_out.at[phase, pl.ds(q, w), pl.ds(first, span)],
            dst_ref=pair_in.at[phase, pl.ds(q, w), pl.ds(first, span)],
            send_sem=pair_send.at[phase],
            recv_sem=pair_recv.at[phase, q, first],
            device_id={"tp": sibling},
            device_id_type=MESH,
        )

    def part_copy(phase, q, target):
        return pltpu.make_async_remote_copy(
            src_ref=part_out.at[phase, q, target],
            dst_ref=part_in.at[phase, q, chip],
            send_sem=rs_send.at[phase],
            recv_sem=rs_recv.at[phase, q],
            device_id={"section": sec + 1 - 2 * phase, "tp": 2 * target + core},
            device_id_type=MESH,
        )

    def rate_copy(q, w):
        return pltpu.make_async_remote_copy(
            src_ref=rate_out.at[pl.ds(q, w)],
            dst_ref=rate_in.at[pl.ds(q, w)],
            send_sem=rate_send,
            recv_sem=rate_recv.at[q],
            device_id={"tp": sibling},
            device_id_type=MESH,
        )

    def vec_copy(target):
        return pltpu.make_async_remote_copy(
            src_ref=vec_out.at[target],
            dst_ref=vec_in.at[chip],
            send_sem=vec_send,
            recv_sem=vec_recv,
            device_id={"tp": 2 * target + core},
            device_id_type=MESH,
        )

    def rows_of(q, w):
        return pl.ds(pl.multiple_of(q * tok, tok), w * tok)

    def stacked(ref, q, w, *rest):
        if rest:
            value = ref[pl.ds(q, w), rest[0]]
        else:
            value = ref[pl.ds(q, w)]
        return value.reshape((w * tok, value.shape[-1]))

    def spread(phase, q, w):
        for k in reversed(range(1, chips)):
            gather_copy(phase, q, w, me, near[k]).start()
        gather_copy(phase, q, w, me, sibling).start()

    def gathered(phase, q, w, consume, enter):
        gather_copy(phase, q, w, sibling, me).wait_recv()
        consume([me, sibling])
        ready = []
        for k in range(1, chips):
            gather_copy(phase, q, w, near[k], me).wait_recv()
            gather_copy(phase, q, w, near[k], sibling).start()
            ready.append(near[k])
            if k > 2:
                gather_copy(phase, q, w, far[k - 2], me).wait_recv()
                ready.append(far[k - 2])
            if k > 1:
                consume(ready)
                ready = []
        enter()
        for k in range(max(1, chips - 2), chips):
            gather_copy(phase, q, w, far[k], me).wait_recv()
            ready.append(far[k])
        if ready:
            consume(ready)

    def reduced(phase, q):
        wait_bytes(part_in.at[phase, q], rs_recv.at[phase, q])
        total = part_in[phase, q, 0].astype(f32)
        for c in range(1, chips):
            total = total + part_in[phase, q, c].astype(f32)
        return total.astype(bf16)

    def enter_forward(q, w):
        @pl.when(sec == 0)
        def _():
            for j in range(w):
                ag[0, q + j, me] = entering_ref[lax.rem(q + j, 2), (q + j) // 2]

        @pl.when(sec > 0)
        def _():
            for j in range(w):
                ag[0, q + j, me] = reduced(0, q + j)

        spread(0, q, w)

    def enter_backward(q, w):
        @pl.when(sec == last)
        def _():
            for j in range(w):
                values = upstream_ref[lax.rem(q + j, 2), (q + j) // 2].astype(f32)
                ag[1, q + j, me] = (values * live_rows[q + j]).astype(bf16)

        @pl.when(sec < last)
        def _():
            for j in range(w):
                ag[1, q + j, me] = reduced(1, q + j)

        spread(1, q, w)

    def scatter(phase, q, w, values_ref, weights, convert, send):
        values = values_ref[rows_of(q, w), :]
        order = list(reversed(range(chips)))
        groups = [order[i : i + span] for i in range(0, chips, span)]

        def product(j):
            return jnp.dot(values, weights[j], preferred_element_type=f32)

        def combine(group, owns):
            pair_copy(phase, q, w, away[group[0]]).wait_recv()
            return [
                own + stacked(pair_in.at[phase], q, w, away[k]).astype(f32)
                for k, own in zip(group, owns)
            ]

        for group in groups:
            for k in group:
                value = product(far[k]).astype(bf16)
                pair_out[phase, pl.ds(q, w), away[k]] = value.reshape((w, tok, width))
            pair_copy(phase, q, w, away[group[0]]).start()
        ahead_owns = [product(near[k]) for k in groups[0]]
        for i, group in enumerate(groups):
            totals = combine(group, ahead_owns)
            if i + 1 < len(groups):
                ahead_owns = [product(near[k]) for k in groups[i + 1]]
            for k, total in zip(group, totals):
                value = convert(k, total).astype(bf16)
                part_out[phase, pl.ds(q, w), away[k]] = value.reshape((w, tok, width))
            send(group)

    def mixed(q, w, source):
        floats = stacked(ag.at[0], q, w, source).astype(f32)
        earlier = pltpu.roll(floats, 1, 0) * stacked(link_ref, q, w)
        delta = earlier - floats
        return floats, delta, floats + mix_ref[source] * delta

    def forward(q, w, enter):
        sums = []

        @pl.when(q == 0)
        def _():
            for j in range(n):
                load_in(j).wait()

            @pl.when(sec < last)
            def _():
                for j in range(n):
                    load_out(j).start()

        def consume(sources):
            for source in sources:
                _, _, united = mixed(q, w, source)
                normed = (united * gain_ref[source]).astype(bf16)
                normed_ref[source, rows_of(q, w), :] = normed
                dots = lax.dot_general(normed, w_in[source], NT, preferred_element_type=f32)
                squares = united * united
                squares = sum(squares[:, c : c + 128] for c in range(0, width, 128))
                if sums:
                    dots, squares = sums[0] + dots, sums[1] + squares
                sums[:] = [dots, squares]

        gathered(0, q, w, consume, enter)
        summed, squares = sums
        summed_ref[rows_of(q, w), :] = summed
        squares = jnp.sum(squares, axis=-1, keepdims=True)
        row_scale = lax.rsqrt(squares / (n * width) + epsilon)
        scale_ref[rows_of(q, w), :] = jnp.broadcast_to(row_scale, (w * tok, 128))
        pre_act = row_scale * summed
        hidden = (pre_act / (1.0 + jnp.exp(-pre_act))).astype(bf16)
        hidden_ref[rows_of(q, w), :] = hidden

    def scatter_forward(q, w):
        @pl.when(q == 0)
        def _():
            for j in range(n):
                load_out(j).wait()

        def convert(k, total):
            return total + stacked(ag.at[0], q, w, me).astype(f32) if k == 0 else total

        def send(group):
            for j in range(w):
                for k in group:
                    part_copy(0, q + j, away[k]).start()

        scatter(0, q, w, hidden_ref, w_out, convert, send)

    def backward(q, w, enter):
        sums = []

        def consume(sources):
            for source in sources:
                values = stacked(ag.at[1], q, w, source)
                up_ref[source, rows_of(q, w), :] = values
                dots = lax.dot_general(values, w_out[source], NT, preferred_element_type=f32)
                sums[:] = [sums[0] + dots if sums else dots]

        gathered(1, q, w, consume, enter)
        hidden_grad[rows_of(q, w), :] = sums[0]

    def scatter_backward(q, w):
        row_scale = scale_ref[rows_of(q, w), :][:, :1]
        summed = summed_ref[rows_of(q, w), :]
        pre_act = row_scale * summed
        sigmoid = 1.0 / (1.0 + jnp.exp(-pre_act))
        gate_grad = hidden_grad[rows_of(q, w), :] * (sigmoid * (1.0 + pre_act * (1.0 - sigmoid)))
        gate_ref[rows_of(q, w), :] = (gate_grad * row_scale).astype(bf16)
        rate = jnp.sum(gate_grad * summed, axis=-1, keepdims=True)
        rate_out[pl.ds(q, w)] = jnp.broadcast_to(rate, (w * tok, 128)).reshape((w, tok, 128))
        rate_copy(q, w).start()
        factors = []

        def convert(k, total):
            if not factors:
                rate_copy(q, w).wait_recv()
                both = stacked(rate_out, q, w)[:, :1] + stacked(rate_in, q, w)[:, :1]
                factors.append(both * (row_scale * row_scale * row_scale) / (n * width))
            target = near[k]
            _, delta, united = mixed(q, w, target)
            mix = mix_ref[target]
            grad_united = total * gain_ref[target] - factors[0] * united
            moved = stacked(link_ref, q, w) * (grad_united * mix)
            below = grad_united * (1.0 - mix) + pltpu.roll(moved, w * tok - 1, 0)
            if k == 0:
                below = below + stacked(ag.at[1], q, w, me).astype(f32)
            gain_rows, mix_rows = total * united, grad_united * delta
            for j in range(w):
                own = slice(j * tok, (j + 1) * tok)
                p = lax.rem(q + j, 2)
                vec_out[away[k], p] += jnp.sum(gain_rows[own], axis=0, keepdims=True)
                vec_out[away[k], 2 + p] += jnp.sum(mix_rows[own], axis=0, keepdims=True)
            return below

        def send(group):
            @pl.when(sec > 0)
            def _():
                for j in range(w):
                    for k in group:
                        part_copy(1, q + j, away[k]).start()

        scatter(1, q, w, gate_ref, w_in, convert, send)

    def runs(plan, enter, work):
        starts = [sum(c * w for c, w in plan[:i]) for i in range(len(plan))]
        for i, (count, w) in enumerate(plan):

            @pl.loop(0, count)
            def _(g, i=i, count=count, w=w):
                q = starts[i] + g * w

                def step():
                    if count > 1:

                        @pl.when(g < count - 1)
                        def _():
                            enter(q + w, w)

                    if i + 1 < len(plan):

                        @pl.when(g == count - 1)
                        def _():
                            enter(starts[i + 1], plan[i + 1][1])

                work(q, w, step)

    @pl.when(sec == last)
    def _():
        @pl.loop(0, packs)
        def _(q):
            enter_backward(q, 1)

        for j in range(n):
            load_out(j).wait()

        @pl.loop(0, packs)
        def _(q):
            backward(q, 1, lambda: None)

    def work_forward(q, w, step):
        forward(q, w, step)

        @pl.when(sec < last)
        def _():
            scatter_forward(q, w)

        @pl.when(sec == last)
        def _():
            scatter_backward(q, w)

    def work_backward(q, w, step):
        backward(q, w, step)
        scatter_backward(q, w)

    enter_forward(0, plans[0][0][1])
    runs(plans[0], enter_forward, work_forward)

    @pl.when(sec < last)
    def _():
        enter_backward(0, plans[1][0][1])
        runs(plans[1], enter_backward, work_backward)

    for k in range(1, chips):
        vec_copy(away[k]).start()
    for phase in range(2):
        wait_bytes(ag.at[phase, :, pl.ds(0, n - 1)], ag_send.at[phase])
    wait_bytes(pair_out.at[1], pair_send.at[1])
    wait_bytes(rate_out, rate_send)

    @pl.when(sec < last)
    def _():
        wait_bytes(pair_out.at[0], pair_send.at[0])
        wait_bytes(part_out.at[0], rs_send.at[0])

    @pl.when(sec > 0)
    def _():
        wait_bytes(part_out.at[1], rs_send.at[1])

    sums = vec_out[chip]
    if chips > 1:
        wait_bytes(vec_in.at[pl.ds(0, chips - 1)], vec_recv)
        for k in range(1, chips):
            sums = sums + vec_in[away[k]]
        wait_bytes(vec_out.at[pl.ds(0, chips - 1)], vec_send)
    vec_sums[...] = sums


def grads_kernel(wide_ref, deep_ref, vec_ref, grad_in, grad_out, gain, mix):
    def summed(left, right):
        return lax.dot_general(left, right, TN, preferred_element_type=jnp.float32)

    def twice_rounded(acc):
        pair = [vec_ref[acc + p].astype(jnp.bfloat16).astype(jnp.float32) for p in range(2)]
        return pair[0] + pair[1]

    grad_in[0] = summed(deep_ref[0], wide_ref[0, 0]).astype(grad_in.dtype)
    grad_out[0] = summed(deep_ref[1], wide_ref[1, 0]).astype(grad_out.dtype)
    gain[...] = twice_rounded(0)
    mix[...] = twice_rounded(2)


def local(
    entering, output_grad, live_counts, segment_ids, weight_in, weight_out, norm_gain, shift_mix
):
    sections = lax.axis_size("section")
    n = lax.axis_size("tp")
    relays, micro, tok, width = entering.shape
    packs = relays * micro
    plans = (FORWARD, BACKWARD)
    hidden = weight_in.shape[2]
    width_all = weight_in.shape[1]
    chips = n // 2
    total = packs * tok
    bf16, f32 = jnp.bfloat16, jnp.float32
    vmem = pl.BlockSpec(memory_space=pltpu.VMEM)
    smem = pl.BlockSpec(memory_space=pltpu.SMEM)
    hbm = pl.BlockSpec(memory_space=pl.ANY)
    dma = pltpu.SemaphoreType.DMA
    wide, deep, vec_sums = pl.pallas_call(
        functools.partial(relay_kernel, n, sections, plans),
        out_shape=(
            jax.ShapeDtypeStruct((2, n, total, width), bf16),
            jax.ShapeDtypeStruct((2, total, hidden), bf16),
            jax.ShapeDtypeStruct((4, 1, width), f32),
        ),
        in_specs=[smem] + [vmem] * 5 + [hbm] * 2,
        out_specs=(vmem,) * 3,
        scratch_shapes=[
            pltpu.VMEM((2, packs, n, tok, width), bf16),
            pltpu.VMEM((2, packs, chips, tok, width), bf16),
            pltpu.VMEM((2, packs, chips, tok, width), bf16),
            pltpu.VMEM((2, packs, chips, tok, width), bf16),
            pltpu.VMEM((2, packs, chips, tok, width), bf16),
            pltpu.VMEM((packs, tok, 1), f32),
            pltpu.VMEM((packs, tok, 1), f32),
            pltpu.VMEM((n, 1, width), f32),
            pltpu.VMEM((n, 1, width), f32),
            pltpu.VMEM((n, hidden, width), bf16),
            pltpu.VMEM((n, hidden, width), bf16),
            pltpu.VMEM((total, hidden), f32),
            pltpu.VMEM((total, hidden), f32),
            pltpu.VMEM((total, 128), f32),
            pltpu.VMEM((packs, tok, 128), f32),
            pltpu.VMEM((packs, tok, 128), f32),
            pltpu.VMEM((chips, 4, 1, width), f32),
            pltpu.VMEM((chips, 4, 1, width), f32),
            dma((2,)),
            dma((2, packs, n)),
            dma((2,)),
            dma((2, packs, chips)),
            dma((2,)),
            dma((2, packs)),
            dma,
            dma((packs,)),
            dma,
            dma,
            dma((2, n)),
        ],
        compiler_params=pltpu.CompilerParams(
            collective_id=0, has_side_effects=True, vmem_limit_bytes=44 * 1024 * 1024
        ),
        name="relays",
    )(
        live_counts,
        entering,
        output_grad,
        jnp.swapaxes(segment_ids, 0, 1),
        norm_gain,
        shift_mix,
        jnp.swapaxes(weight_in[0], 0, 1),
        weight_out[0],
    )

    part = pl.BlockSpec((2, 1, total, width), lambda j: (0, j, 0, 0))
    whole = pl.BlockSpec((2, total, hidden), lambda j: (0, 0, 0))
    sums = pl.BlockSpec((4, 1, width), lambda j: (0, 0, 0))
    row = pl.BlockSpec((1, width), lambda j: (0, 0))
    grad_in, grad_out, gain, mix = pl.pallas_call(
        grads_kernel,
        grid=(n,),
        out_shape=(
            jax.ShapeDtypeStruct((1, hidden, width_all), bf16),
            jax.ShapeDtypeStruct((1, hidden, width_all), bf16),
            jax.ShapeDtypeStruct((1, width), f32),
            jax.ShapeDtypeStruct((1, width), f32),
        ),
        in_specs=[part, whole, sums],
        out_specs=(
            pl.BlockSpec((1, hidden, width), lambda j: (0, 0, j)),
            pl.BlockSpec((1, hidden, width), lambda j: (0, 0, j)),
            row,
            row,
        ),
        compiler_params=pltpu.CompilerParams(
            dimension_semantics=("arbitrary",), vmem_limit_bytes=24 * 1024 * 1024
        ),
        name="weight_grads",
    )(wide, deep, vec_sums)
    return jnp.swapaxes(grad_in, 1, 2), grad_out, gain, mix


def solution(mesh):
    in_specs = (
        P(None, None, None, "tp"),
        P(None, None, None, "tp"),
        P(),
        P(),
        P("section", None, "tp"),
        P("section", "tp", None),
        P("section", None),
        P("section", None),
    )
    out_specs = (
        P("section", None, "tp"),
        P("section", "tp", None),
        P("section", "tp"),
        P("section", "tp"),
    )
    return jax.shard_map(local, mesh=mesh, in_specs=in_specs, out_specs=out_specs, check_vma=False)
```

```python
import functools

import jax
import jax.numpy as jnp
from jax import lax
from jax.experimental import pallas as pl
from jax.experimental.pallas import tpu as pltpu
from jax.sharding import PartitionSpec as P

epsilon = 1e-05
MESH = pl.DeviceIdType.MESH
NT = (((1,), (1,)), ((), ()))
TN = (((0,), (0,)), ((), ()))
FORWARD = ((6, 1),)
BACKWARD = ((6, 1),)


def wait_bytes(ref, sem):
    pltpu.make_async_copy(ref, ref, sem).wait()


def relay_kernel(
    n,
    sections,
    plans,
    live_ref,
    entering_ref,
    upstream_ref,
    segment_ref,
    gain_row,
    mix_row,
    w_in_hbm,
    w_out_hbm,
    wide_ref,
    deep_ref,
    vec_sums,
    ag,
    pair_out,
    pair_in,
    part_out,
    part_in,
    link_ref,
    live_rows,
    gain_ref,
    mix_ref,
    w_in,
    w_out,
    summed_ref,
    hidden_grad,
    scale_ref,
    rate_out,
    rate_in,
    vec_out,
    vec_in,
    ag_send,
    ag_recv,
    pair_send,
    pair_recv,
    rs_send,
    rs_recv,
    rate_send,
    rate_recv,
    vec_send,
    vec_recv,
    w_sem,
):
    me = lax.axis_index("tp")
    sec = lax.axis_index("section")
    _, micro, tok, width = entering_ref.shape
    packs = 2 * micro
    normed_ref, up_ref = wide_ref.at[0], wide_ref.at[1]
    gate_ref, hidden_ref = deep_ref.at[0], deep_ref.at[1]
    chips = n // 2
    chip = me // 2
    core = lax.rem(me, 2)
    sibling = me + 1 - 2 * core
    last = sections - 1
    bf16, f32 = jnp.bfloat16, jnp.float32

    def chip_at(k):
        value, bit = chip, 1
        while bit <= k:
            if k & bit:
                value = value + bit - 2 * bit * lax.rem(chip // bit, 2)
            bit *= 2
        return value

    away = [chip_at(k) for k in range(chips)]
    span = min(2, chips)
    near = [2 * c + core for c in away]
    far = [2 * c + 1 - core for c in away]

    barrier = pltpu.get_barrier_semaphore()

    def greet(**device):
        pl.semaphore_signal(barrier, inc=1, device_id=device, device_id_type=MESH)

    for k in range(1, chips):
        greet(tp=near[k])
    greet(tp=sibling)

    @pl.when(sec > 0)
    def _():
        for k in range(chips):
            greet(section=sec - 1, tp=near[k])

    @pl.when(sec < last)
    def _():
        for k in range(chips):
            greet(section=sec + 1, tp=near[k])

    def load_in(j):
        return pltpu.make_async_copy(
            w_in_hbm.at[:, pl.ds(pl.multiple_of(j * width, width), width)],
            w_in.at[j],
            w_sem.at[0, j],
        )

    def load_out(j):
        return pltpu.make_async_copy(
            w_out_hbm.at[:, pl.ds(pl.multiple_of(j * width, width), width)],
            w_out.at[j],
            w_sem.at[1, j],
        )

    @pl.when(sec == last)
    def _():
        for j in range(n):
            load_out(j).start()

    for j in range(n):
        load_in(j).start()

    square = [lax.broadcasted_iota(jnp.int32, (tok, tok), axis) for axis in range(2)]
    column = lax.broadcasted_iota(jnp.int32, (tok, 1), 0)
    for p in range(2):
        for m in range(micro):
            ids = segment_ref[m, p : p + 1, :].astype(f32)
            here = jnp.sum(jnp.where(square[0] == square[1], ids, 0.0), axis=-1, keepdims=True)
            before = jnp.sum(
                jnp.where(square[0] == square[1] + 1, ids, 0.0), axis=-1, keepdims=True
            )
            joined = jnp.logical_and(here == before, column > 0)
            link_ref[2 * m + p] = jnp.where(joined, 1.0, 0.0)
            live_rows[2 * m + p] = jnp.where(column < live_ref[p, m], 1.0, 0.0)
    for j in range(n):
        own = slice(j * width, (j + 1) * width)
        gain_ref[j] = gain_row[:, own].astype(f32)
        mix_ref[j] = mix_row[:, own].astype(f32)
    vec_out[...] = jnp.zeros_like(vec_out)

    outer = jnp.logical_or(sec == 0, sec == last)

    @pl.when(outer)
    def _():
        pl.semaphore_wait(barrier, 2 * chips)

    @pl.when(jnp.logical_not(outer))
    def _():
        pl.semaphore_wait(barrier, 3 * chips)

    def gather_copy(phase, q, w, source, peer):
        return pltpu.make_async_remote_copy(
            src_ref=ag.at[phase, pl.ds(q, w), source],
            dst_ref=ag.at[phase, pl.ds(q, w), source],
            send_sem=ag_send.at[phase],
            recv_sem=ag_recv.at[phase, q, source],
            device_id={"tp": peer},
            device_id_type=MESH,
        )

    def pair_copy(phase, q, w, target):
        first = target - lax.rem(target, span)
        return pltpu.make_async_remote_copy(
            src_ref=pair_out.at[phase, pl.ds(q, w), pl.ds(first, span)],
            dst_ref=pair_in.at[phase, pl.ds(q, w), pl.ds(first, span)],
            send_sem=pair_send.at[phase],
            recv_sem=pair_recv.at[phase, q, first],
            device_id={"tp": sibling},
            device_id_type=MESH,
        )

    def part_copy(phase, q, target):
        return pltpu.make_async_remote_copy(
            src_ref=part_out.at[phase, q, target],
            dst_ref=part_in.at[phase, q, chip],
            send_sem=rs_send.at[phase],
            recv_sem=rs_recv.at[phase, q],
            device_id={"section": sec + 1 - 2 * phase, "tp": 2 * target + core},
            device_id_type=MESH,
        )

    def rate_copy(q, w):
        return pltpu.make_async_remote_copy(
            src_ref=rate_out.at[pl.ds(q, w)],
            dst_ref=rate_in.at[pl.ds(q, w)],
            send_sem=rate_send,
            recv_sem=rate_recv.at[q],
            device_id={"tp": sibling},
            device_id_type=MESH,
        )

    def vec_copy(target):
        return pltpu.make_async_remote_copy(
            src_ref=vec_out.at[target],
            dst_ref=vec_in.at[chip],
            send_sem=vec_send,
            recv_sem=vec_recv,
            device_id={"tp": 2 * target + core},
            device_id_type=MESH,
        )

    def rows_of(q, w):
        return pl.ds(pl.multiple_of(q * tok, tok), w * tok)

    def stacked(ref, q, w, *rest):
        if rest:
            value = ref[pl.ds(q, w), rest[0]]
        else:
            value = ref[pl.ds(q, w)]
        return value.reshape((w * tok, value.shape[-1]))

    def spread(phase, q, w):
        for k in reversed(range(1, chips)):
            gather_copy(phase, q, w, me, near[k]).start()
        gather_copy(phase, q, w, me, sibling).start()

    def gathered(phase, q, w, consume, enter):
        gather_copy(phase, q, w, sibling, me).wait_recv()
        consume([me, sibling])
        ready = []
        for k in range(1, chips):
            gather_copy(phase, q, w, near[k], me).wait_recv()
            gather_copy(phase, q, w, near[k], sibling).start()
            ready.append(near[k])
            if k > 2:
                gather_copy(phase, q, w, far[k - 2], me).wait_recv()
                ready.append(far[k - 2])
            if k > 1:
                consume(ready)
                ready = []
        enter()
        for k in range(max(1, chips - 2), chips):
            gather_copy(phase, q, w, far[k], me).wait_recv()
            ready.append(far[k])
        if ready:
            consume(ready)

    def reduced(phase, q):
        wait_bytes(part_in.at[phase, q], rs_recv.at[phase, q])
        total = part_in[phase, q, 0].astype(f32)
        for c in range(1, chips):
            total = total + part_in[phase, q, c].astype(f32)
        return total.astype(bf16)

    def enter_forward(q, w):
        @pl.when(sec == 0)
        def _():
            for j in range(w):
                ag[0, q + j, me] = entering_ref[lax.rem(q + j, 2), (q + j) // 2]

        @pl.when(sec > 0)
        def _():
            for j in range(w):
                ag[0, q + j, me] = reduced(0, q + j)

        spread(0, q, w)

    def enter_backward(q, w):
        @pl.when(sec == last)
        def _():
            for j in range(w):
                values = upstream_ref[lax.rem(q + j, 2), (q + j) // 2].astype(f32)
                ag[1, q + j, me] = (values * live_rows[q + j]).astype(bf16)

        @pl.when(sec < last)
        def _():
            for j in range(w):
                ag[1, q + j, me] = reduced(1, q + j)

        spread(1, q, w)

    def scatter(phase, q, w, values_ref, weights, beside, convert, send):
        values = values_ref[rows_of(q, w), :]
        order = list(reversed(range(chips)))
        groups = [order[i : i + span] for i in range(0, chips, span)]

        def product(j):
            return jnp.dot(values, weights[j], preferred_element_type=f32)

        def combine(group, owns):
            pair_copy(phase, q, w, away[group[0]]).wait_recv()
            return [
                own + stacked(pair_in.at[phase], q, w, away[k]).astype(f32)
                for k, own in zip(group, owns)
            ]

        for group in groups:
            for k in group:
                value = product(far[k]).astype(bf16)
                pair_out[phase, pl.ds(q, w), away[k]] = value.reshape((w, tok, width))
            if group is groups[0]:
                beside()
            pair_copy(phase, q, w, away[group[0]]).start()
        ahead_owns = [product(near[k]) for k in groups[0]]
        for i, group in enumerate(groups):
            totals = combine(group, ahead_owns)
            if i + 1 < len(groups):
                ahead_owns = [product(near[k]) for k in groups[i + 1]]
            for k, total in zip(group, totals):
                value = convert(k, total).astype(bf16)
                part_out[phase, pl.ds(q, w), away[k]] = value.reshape((w, tok, width))
            send(group)

    def mixed(q, w, source):
        floats = stacked(ag.at[0], q, w, source).astype(f32)
        earlier = pltpu.roll(floats, 1, 0) * stacked(link_ref, q, w)
        delta = earlier - floats
        return floats, delta, floats + mix_ref[source] * delta

    def forward(q, w, enter):
        sums = []

        @pl.when(q == 0)
        def _():
            for j in range(n):
                load_in(j).wait()

            @pl.when(sec < last)
            def _():
                for j in range(n):
                    load_out(j).start()

        def consume(sources):
            for source in sources:
                _, _, united = mixed(q, w, source)
                normed = (united * gain_ref[source]).astype(bf16)
                normed_ref[source, rows_of(q, w), :] = normed
                dots = lax.dot_general(normed, w_in[source], NT, preferred_element_type=f32)
                squares = united * united
                squares = sum(squares[:, c : c + 128] for c in range(0, width, 128))
                if sums:
                    dots, squares = sums[0] + dots, sums[1] + squares
                sums[:] = [dots, squares]

        gathered(0, q, w, consume, enter)
        summed, squares = sums
        summed_ref[rows_of(q, w), :] = summed
        squares = jnp.sum(squares, axis=-1, keepdims=True)
        row_scale = lax.rsqrt(squares / (n * width) + epsilon)
        scale_ref[rows_of(q, w), :] = jnp.broadcast_to(row_scale, (w * tok, 128))
        pre_act = row_scale * summed
        hidden = (pre_act / (1.0 + jnp.exp(-pre_act))).astype(bf16)
        hidden_ref[rows_of(q, w), :] = hidden

    def scatter_forward(q, w):
        @pl.when(q == 0)
        def _():
            for j in range(n):
                load_out(j).wait()

        def convert(k, total):
            return total + stacked(ag.at[0], q, w, me).astype(f32) if k == 0 else total

        def send(group):
            for j in range(w):
                for k in group:
                    part_copy(0, q + j, away[k]).start()

        scatter(0, q, w, hidden_ref, w_out, lambda: None, convert, send)

    def backward(q, w, enter):
        sums = []

        def consume(sources):
            for source in sources:
                values = stacked(ag.at[1], q, w, source)
                up_ref[source, rows_of(q, w), :] = values
                dots = lax.dot_general(values, w_out[source], NT, preferred_element_type=f32)
                sums[:] = [sums[0] + dots if sums else dots]

        gathered(1, q, w, consume, enter)
        hidden_grad[rows_of(q, w), :] = sums[0]

    def scatter_backward(q, w):
        row_scale = scale_ref[rows_of(q, w), :][:, :1]
        summed = summed_ref[rows_of(q, w), :]
        pre_act = row_scale * summed
        sigmoid = 1.0 / (1.0 + jnp.exp(-pre_act))
        gate_grad = hidden_grad[rows_of(q, w), :] * (sigmoid * (1.0 + pre_act * (1.0 - sigmoid)))
        gate_ref[rows_of(q, w), :] = (gate_grad * row_scale).astype(bf16)
        factors = []
        pending = []

        def beside():
            rate = jnp.sum(gate_grad * summed, axis=-1, keepdims=True)
            rate_out[pl.ds(q, w)] = jnp.broadcast_to(rate, (w * tok, 128)).reshape((w, tok, 128))
            rate_copy(q, w).start()

        def convert(k, total):
            if not factors:
                rate_copy(q, w).wait_recv()
                both = stacked(rate_out, q, w)[:, :1] + stacked(rate_in, q, w)[:, :1]
                factors.append(both * (row_scale * row_scale * row_scale) / (n * width))
            target = near[k]
            _, delta, united = mixed(q, w, target)
            mix = mix_ref[target]
            grad_united = total * gain_ref[target] - factors[0] * united
            moved = stacked(link_ref, q, w) * (grad_united * mix)
            below = grad_united * (1.0 - mix) + pltpu.roll(moved, w * tok - 1, 0)
            if k == 0:
                below = below + stacked(ag.at[1], q, w, me).astype(f32)
            pending.append((k, total * united, grad_united * delta))
            return below

        def send(group):
            @pl.when(sec > 0)
            def _():
                for j in range(w):
                    for k in group:
                        part_copy(1, q + j, away[k]).start()

            for k, gain_rows, mix_rows in pending:
                for j in range(w):
                    own = slice(j * tok, (j + 1) * tok)
                    p = lax.rem(q + j, 2)
                    vec_out[away[k], p] += jnp.sum(gain_rows[own], axis=0, keepdims=True)
                    vec_out[away[k], 2 + p] += jnp.sum(mix_rows[own], axis=0, keepdims=True)
            pending.clear()

            @pl.when(q + w == packs)
            def _():
                for k in group:
                    if k > 0:
                        vec_copy(away[k]).start()

        scatter(1, q, w, gate_ref, w_in, beside, convert, send)

    def runs(plan, enter, work):
        starts = [sum(c * w for c, w in plan[:i]) for i in range(len(plan))]
        for i, (count, w) in enumerate(plan):

            @pl.loop(0, count)
            def _(g, i=i, count=count, w=w):
                q = starts[i] + g * w

                def step():
                    if count > 1:

                        @pl.when(g < count - 1)
                        def _():
                            enter(q + w, w)

                    if i + 1 < len(plan):

                        @pl.when(g == count - 1)
                        def _():
                            enter(starts[i + 1], plan[i + 1][1])

                work(q, w, step)

    @pl.when(sec == last)
    def _():
        @pl.loop(0, packs)
        def _(q):
            enter_backward(q, 1)

        for j in range(n):
            load_out(j).wait()

        @pl.loop(0, packs)
        def _(q):
            backward(q, 1, lambda: None)

    def work_forward(q, w, step):
        forward(q, w, step)

        @pl.when(sec < last)
        def _():
            scatter_forward(q, w)

        @pl.when(sec == last)
        def _():
            scatter_backward(q, w)

    def work_backward(q, w, step):
        backward(q, w, step)
        scatter_backward(q, w)

    enter_forward(0, plans[0][0][1])
    runs(plans[0], enter_forward, work_forward)

    @pl.when(sec < last)
    def _():
        enter_backward(0, plans[1][0][1])
        runs(plans[1], enter_backward, work_backward)

    for phase in range(2):
        wait_bytes(ag.at[phase, :, pl.ds(0, n - 1)], ag_send.at[phase])
    wait_bytes(pair_out.at[1], pair_send.at[1])
    wait_bytes(rate_out, rate_send)

    @pl.when(sec < last)
    def _():
        wait_bytes(pair_out.at[0], pair_send.at[0])
        wait_bytes(part_out.at[0], rs_send.at[0])

    @pl.when(sec > 0)
    def _():
        wait_bytes(part_out.at[1], rs_send.at[1])

    sums = vec_out[chip]
    if chips > 1:
        wait_bytes(vec_in.at[pl.ds(0, chips - 1)], vec_recv)
        for k in range(1, chips):
            sums = sums + vec_in[away[k]]
        wait_bytes(vec_out.at[pl.ds(0, chips - 1)], vec_send)
    vec_sums[...] = sums


def grads_kernel(wide_ref, deep_ref, vec_ref, grad_in, grad_out, gain, mix):
    def summed(left, right):
        return lax.dot_general(left, right, TN, preferred_element_type=jnp.float32)

    def twice_rounded(acc):
        pair = [vec_ref[acc + p].astype(jnp.bfloat16).astype(jnp.float32) for p in range(2)]
        return pair[0] + pair[1]

    grad_in[0] = summed(deep_ref[0], wide_ref[0, 0]).astype(grad_in.dtype)
    grad_out[0] = summed(deep_ref[1], wide_ref[1, 0]).astype(grad_out.dtype)
    gain[...] = twice_rounded(0)
    mix[...] = twice_rounded(2)


def local(
    entering, output_grad, live_counts, segment_ids, weight_in, weight_out, norm_gain, shift_mix
):
    sections = lax.axis_size("section")
    n = lax.axis_size("tp")
    relays, micro, tok, width = entering.shape
    packs = relays * micro
    plans = (FORWARD, BACKWARD)
    hidden = weight_in.shape[2]
    width_all = weight_in.shape[1]
    chips = n // 2
    total = packs * tok
    bf16, f32 = jnp.bfloat16, jnp.float32
    vmem = pl.BlockSpec(memory_space=pltpu.VMEM)
    smem = pl.BlockSpec(memory_space=pltpu.SMEM)
    hbm = pl.BlockSpec(memory_space=pl.ANY)
    dma = pltpu.SemaphoreType.DMA
    wide, deep, vec_sums = pl.pallas_call(
        functools.partial(relay_kernel, n, sections, plans),
        out_shape=(
            jax.ShapeDtypeStruct((2, n, total, width), bf16),
            jax.ShapeDtypeStruct((2, total, hidden), bf16),
            jax.ShapeDtypeStruct((4, 1, width), f32),
        ),
        in_specs=[smem] + [vmem] * 5 + [hbm] * 2,
        out_specs=(vmem,) * 3,
        scratch_shapes=[
            pltpu.VMEM((2, packs, n, tok, width), bf16),
            pltpu.VMEM((2, packs, chips, tok, width), bf16),
            pltpu.VMEM((2, packs, chips, tok, width), bf16),
            pltpu.VMEM((2, packs, chips, tok, width), bf16),
            pltpu.VMEM((2, packs, chips, tok, width), bf16),
            pltpu.VMEM((packs, tok, 1), f32),
            pltpu.VMEM((packs, tok, 1), f32),
            pltpu.VMEM((n, 1, width), f32),
            pltpu.VMEM((n, 1, width), f32),
            pltpu.VMEM((n, hidden, width), bf16),
            pltpu.VMEM((n, hidden, width), bf16),
            pltpu.VMEM((total, hidden), f32),
            pltpu.VMEM((total, hidden), f32),
            pltpu.VMEM((total, 128), f32),
            pltpu.VMEM((packs, tok, 128), f32),
            pltpu.VMEM((packs, tok, 128), f32),
            pltpu.VMEM((chips, 4, 1, width), f32),
            pltpu.VMEM((chips, 4, 1, width), f32),
            dma((2,)),
            dma((2, packs, n)),
            dma((2,)),
            dma((2, packs, chips)),
            dma((2,)),
            dma((2, packs)),
            dma,
            dma((packs,)),
            dma,
            dma,
            dma((2, n)),
        ],
        compiler_params=pltpu.CompilerParams(
            collective_id=0, has_side_effects=True, vmem_limit_bytes=44 * 1024 * 1024
        ),
        name="relays",
    )(
        live_counts,
        entering,
        output_grad,
        jnp.swapaxes(segment_ids, 0, 1),
        norm_gain,
        shift_mix,
        jnp.swapaxes(weight_in[0], 0, 1),
        weight_out[0],
    )

    part = pl.BlockSpec((2, 1, total, width), lambda j: (0, j, 0, 0))
    whole = pl.BlockSpec((2, total, hidden), lambda j: (0, 0, 0))
    sums = pl.BlockSpec((4, 1, width), lambda j: (0, 0, 0))
    row = pl.BlockSpec((1, width), lambda j: (0, 0))
    grad_in, grad_out, gain, mix = pl.pallas_call(
        grads_kernel,
        grid=(n,),
        out_shape=(
            jax.ShapeDtypeStruct((1, hidden, width_all), bf16),
            jax.ShapeDtypeStruct((1, hidden, width_all), bf16),
            jax.ShapeDtypeStruct((1, width), f32),
            jax.ShapeDtypeStruct((1, width), f32),
        ),
        in_specs=[part, whole, sums],
        out_specs=(
            pl.BlockSpec((1, hidden, width), lambda j: (0, 0, j)),
            pl.BlockSpec((1, hidden, width), lambda j: (0, 0, j)),
            row,
            row,
        ),
        compiler_params=pltpu.CompilerParams(
            dimension_semantics=("arbitrary",), vmem_limit_bytes=24 * 1024 * 1024
        ),
        name="weight_grads",
    )(wide, deep, vec_sums)
    return jnp.swapaxes(grad_in, 1, 2), grad_out, gain, mix


def solution(mesh):
    in_specs = (
        P(None, None, None, "tp"),
        P(None, None, None, "tp"),
        P(),
        P(),
        P("section", None, "tp"),
        P("section", "tp", None),
        P("section", None),
        P("section", None),
    )
    out_specs = (
        P("section", None, "tp"),
        P("section", "tp", None),
        P("section", "tp"),
        P("section", "tp"),
    )
    return jax.shard_map(local, mesh=mesh, in_specs=in_specs, out_specs=out_specs, check_vma=False)
```

```python
import functools

import jax
import jax.numpy as jnp
from jax import lax
from jax.experimental import pallas as pl
from jax.experimental.pallas import tpu as pltpu
from jax.sharding import PartitionSpec as P

epsilon = 1e-05
MESH = pl.DeviceIdType.MESH
NT = (((1,), (1,)), ((), ()))
TN = (((0,), (0,)), ((), ()))
FORWARD = ((6, 1),)
BACKWARD = ((6, 1),)


def wait_bytes(ref, sem):
    pltpu.make_async_copy(ref, ref, sem).wait()


def relay_kernel(
    n,
    sections,
    plans,
    live_ref,
    entering_ref,
    upstream_ref,
    segment_ref,
    gain_row,
    mix_row,
    w_in_hbm,
    w_out_hbm,
    wide_ref,
    deep_ref,
    vec_sums,
    ag,
    pair_out,
    pair_in,
    part_out,
    part_in,
    link_ref,
    live_rows,
    gain_ref,
    mix_ref,
    w_in,
    w_out,
    summed_ref,
    hidden_grad,
    slope_ref,
    scale_ref,
    rate_out,
    rate_in,
    vec_out,
    vec_in,
    ag_send,
    ag_recv,
    pair_send,
    pair_recv,
    rs_send,
    rs_recv,
    rate_send,
    rate_recv,
    vec_send,
    vec_recv,
    w_sem,
):
    me = lax.axis_index("tp")
    sec = lax.axis_index("section")
    _, micro, tok, width = entering_ref.shape
    packs = 2 * micro
    normed_ref, up_ref = wide_ref.at[0], wide_ref.at[1]
    gate_ref, hidden_ref = deep_ref.at[0], deep_ref.at[1]
    chips = n // 2
    chip = me // 2
    core = lax.rem(me, 2)
    sibling = me + 1 - 2 * core
    last = sections - 1
    bf16, f32 = jnp.bfloat16, jnp.float32

    def chip_at(k):
        value, bit = chip, 1
        while bit <= k:
            if k & bit:
                value = value + bit - 2 * bit * lax.rem(chip // bit, 2)
            bit *= 2
        return value

    away = [chip_at(k) for k in range(chips)]
    span = min(2, chips)
    near = [2 * c + core for c in away]
    far = [2 * c + 1 - core for c in away]

    barrier = pltpu.get_barrier_semaphore()

    def greet(**device):
        pl.semaphore_signal(barrier, inc=1, device_id=device, device_id_type=MESH)

    for k in range(1, chips):
        greet(tp=near[k])
    greet(tp=sibling)

    @pl.when(sec > 0)
    def _():
        for k in range(chips):
            greet(section=sec - 1, tp=near[k])

    @pl.when(sec < last)
    def _():
        for k in range(chips):
            greet(section=sec + 1, tp=near[k])

    def load_in(j):
        return pltpu.make_async_copy(
            w_in_hbm.at[:, pl.ds(pl.multiple_of(j * width, width), width)],
            w_in.at[j],
            w_sem.at[0, j],
        )

    def load_out(j):
        return pltpu.make_async_copy(
            w_out_hbm.at[:, pl.ds(pl.multiple_of(j * width, width), width)],
            w_out.at[j],
            w_sem.at[1, j],
        )

    @pl.when(sec == last)
    def _():
        for j in range(n):
            load_out(j).start()

    for j in range(n):
        load_in(j).start()

    square = [lax.broadcasted_iota(jnp.int32, (tok, tok), axis) for axis in range(2)]
    column = lax.broadcasted_iota(jnp.int32, (tok, 1), 0)
    for p in range(2):
        for m in range(micro):
            ids = segment_ref[m, p : p + 1, :].astype(f32)
            here = jnp.sum(jnp.where(square[0] == square[1], ids, 0.0), axis=-1, keepdims=True)
            before = jnp.sum(
                jnp.where(square[0] == square[1] + 1, ids, 0.0), axis=-1, keepdims=True
            )
            joined = jnp.logical_and(here == before, column > 0)
            link_ref[2 * m + p] = jnp.where(joined, 1.0, 0.0)
            live_rows[2 * m + p] = jnp.where(column < live_ref[p, m], 1.0, 0.0)
    for j in range(n):
        own = slice(j * width, (j + 1) * width)
        gain_ref[j] = gain_row[:, own].astype(f32)
        mix_ref[j] = mix_row[:, own].astype(f32)
    vec_out[...] = jnp.zeros_like(vec_out)

    outer = jnp.logical_or(sec == 0, sec == last)

    @pl.when(outer)
    def _():
        pl.semaphore_wait(barrier, 2 * chips)

    @pl.when(jnp.logical_not(outer))
    def _():
        pl.semaphore_wait(barrier, 3 * chips)

    def gather_copy(phase, q, w, source, peer):
        return pltpu.make_async_remote_copy(
            src_ref=ag.at[phase, pl.ds(q, w), source],
            dst_ref=ag.at[phase, pl.ds(q, w), source],
            send_sem=ag_send.at[phase],
            recv_sem=ag_recv.at[phase, q, source],
            device_id={"tp": peer},
            device_id_type=MESH,
        )

    def pair_copy(phase, q, w, target):
        first = target - lax.rem(target, span)
        return pltpu.make_async_remote_copy(
            src_ref=pair_out.at[phase, pl.ds(q, w), pl.ds(first, span)],
            dst_ref=pair_in.at[phase, pl.ds(q, w), pl.ds(first, span)],
            send_sem=pair_send.at[phase],
            recv_sem=pair_recv.at[phase, q, first],
            device_id={"tp": sibling},
            device_id_type=MESH,
        )

    def part_copy(phase, q, target):
        return pltpu.make_async_remote_copy(
            src_ref=part_out.at[phase, q, target],
            dst_ref=part_in.at[phase, q, chip],
            send_sem=rs_send.at[phase],
            recv_sem=rs_recv.at[phase, q],
            device_id={"section": sec + 1 - 2 * phase, "tp": 2 * target + core},
            device_id_type=MESH,
        )

    def rate_copy(q, w):
        return pltpu.make_async_remote_copy(
            src_ref=rate_out.at[pl.ds(q, w)],
            dst_ref=rate_in.at[pl.ds(q, w)],
            send_sem=rate_send,
            recv_sem=rate_recv.at[q],
            device_id={"tp": sibling},
            device_id_type=MESH,
        )

    def vec_copy(target):
        return pltpu.make_async_remote_copy(
            src_ref=vec_out.at[target],
            dst_ref=vec_in.at[chip],
            send_sem=vec_send,
            recv_sem=vec_recv,
            device_id={"tp": 2 * target + core},
            device_id_type=MESH,
        )

    def rows_of(q, w):
        return pl.ds(pl.multiple_of(q * tok, tok), w * tok)

    def stacked(ref, q, w, *rest):
        if rest:
            value = ref[pl.ds(q, w), rest[0]]
        else:
            value = ref[pl.ds(q, w)]
        return value.reshape((w * tok, value.shape[-1]))

    def spread(phase, q, w):
        for k in reversed(range(1, chips)):
            gather_copy(phase, q, w, me, near[k]).start()
        gather_copy(phase, q, w, me, sibling).start()

    def gathered(phase, q, w, consume, enter):
        gather_copy(phase, q, w, sibling, me).wait_recv()
        consume([me, sibling])
        ready = []
        for k in range(1, chips):
            gather_copy(phase, q, w, near[k], me).wait_recv()
            gather_copy(phase, q, w, near[k], sibling).start()
            ready.append(near[k])
            if k > 2:
                gather_copy(phase, q, w, far[k - 2], me).wait_recv()
                ready.append(far[k - 2])
            if k > 1:
                consume(ready)
                ready = []
        enter()
        for k in range(max(1, chips - 2), chips):
            gather_copy(phase, q, w, far[k], me).wait_recv()
            ready.append(far[k])
        if ready:
            consume(ready)

    def reduced(phase, q):
        wait_bytes(part_in.at[phase, q], rs_recv.at[phase, q])
        total = part_in[phase, q, 0].astype(f32)
        for c in range(1, chips):
            total = total + part_in[phase, q, c].astype(f32)
        return total.astype(bf16)

    def enter_forward(q, w):
        @pl.when(sec == 0)
        def _():
            for j in range(w):
                ag[0, q + j, me] = entering_ref[lax.rem(q + j, 2), (q + j) // 2]

        @pl.when(sec > 0)
        def _():
            for j in range(w):
                ag[0, q + j, me] = reduced(0, q + j)

        spread(0, q, w)

    def enter_backward(q, w):
        @pl.when(sec == last)
        def _():
            for j in range(w):
                values = upstream_ref[lax.rem(q + j, 2), (q + j) // 2].astype(f32)
                ag[1, q + j, me] = (values * live_rows[q + j]).astype(bf16)

        @pl.when(sec < last)
        def _():
            for j in range(w):
                ag[1, q + j, me] = reduced(1, q + j)

        spread(1, q, w)

    def scatter(phase, q, w, values_ref, weights, beside, convert, send):
        values = values_ref[rows_of(q, w), :]
        order = list(reversed(range(chips)))
        groups = [order[i : i + span] for i in range(0, chips, span)]

        def product(j):
            return jnp.dot(values, weights[j], preferred_element_type=f32)

        def combine(group, owns):
            pair_copy(phase, q, w, away[group[0]]).wait_recv()
            return [
                own + stacked(pair_in.at[phase], q, w, away[k]).astype(f32)
                for k, own in zip(group, owns)
            ]

        for group in groups:
            for k in group:
                value = product(far[k]).astype(bf16)
                pair_out[phase, pl.ds(q, w), away[k]] = value.reshape((w, tok, width))
            if group is groups[0]:
                beside()
            pair_copy(phase, q, w, away[group[0]]).start()
        ahead_owns = [product(near[k]) for k in groups[0]]
        for i, group in enumerate(groups):
            totals = combine(group, ahead_owns)
            if i + 1 < len(groups):
                ahead_owns = [product(near[k]) for k in groups[i + 1]]
            for k, total in zip(group, totals):
                value = convert(k, total).astype(bf16)
                part_out[phase, pl.ds(q, w), away[k]] = value.reshape((w, tok, width))
            send(group)

    def mixed(q, w, source):
        floats = stacked(ag.at[0], q, w, source).astype(f32)
        earlier = pltpu.roll(floats, 1, 0) * stacked(link_ref, q, w)
        delta = earlier - floats
        return floats, delta, floats + mix_ref[source] * delta

    def forward(q, w, enter):
        sums = []

        @pl.when(q == 0)
        def _():
            for j in range(n):
                load_in(j).wait()

            @pl.when(sec < last)
            def _():
                for j in range(n):
                    load_out(j).start()

        def consume(sources):
            for source in sources:
                _, _, united = mixed(q, w, source)
                normed = (united * gain_ref[source]).astype(bf16)
                normed_ref[source, rows_of(q, w), :] = normed
                dots = lax.dot_general(normed, w_in[source], NT, preferred_element_type=f32)
                squares = united * united
                squares = sum(squares[:, c : c + 128] for c in range(0, width, 128))
                if sums:
                    dots, squares = sums[0] + dots, sums[1] + squares
                sums[:] = [dots, squares]

        gathered(0, q, w, consume, enter)
        summed, squares = sums
        summed_ref[rows_of(q, w), :] = summed
        squares = jnp.sum(squares, axis=-1, keepdims=True)
        row_scale = lax.rsqrt(squares / (n * width) + epsilon)
        scale_ref[rows_of(q, w), :] = jnp.broadcast_to(row_scale, (w * tok, 128))
        pre_act = row_scale * summed
        sigmoid = 1.0 / (1.0 + jnp.exp(-pre_act))
        hidden_ref[rows_of(q, w), :] = (pre_act * sigmoid).astype(bf16)
        slope_ref[rows_of(q, w), :] = sigmoid * (1.0 + pre_act * (1.0 - sigmoid))

    def scatter_forward(q, w):
        @pl.when(q == 0)
        def _():
            for j in range(n):
                load_out(j).wait()

        def convert(k, total):
            return total + stacked(ag.at[0], q, w, me).astype(f32) if k == 0 else total

        def send(group):
            for j in range(w):
                for k in group:
                    part_copy(0, q + j, away[k]).start()

        scatter(0, q, w, hidden_ref, w_out, lambda: None, convert, send)

    def backward(q, w, enter):
        sums = []

        def consume(sources):
            for source in sources:
                values = stacked(ag.at[1], q, w, source)
                up_ref[source, rows_of(q, w), :] = values
                dots = lax.dot_general(values, w_out[source], NT, preferred_element_type=f32)
                sums[:] = [sums[0] + dots if sums else dots]

        gathered(1, q, w, consume, enter)
        hidden_grad[rows_of(q, w), :] = sums[0]

    def scatter_backward(q, w):
        row_scale = scale_ref[rows_of(q, w), :][:, :1]
        summed = summed_ref[rows_of(q, w), :]
        gate_grad = hidden_grad[rows_of(q, w), :] * slope_ref[rows_of(q, w), :]
        gate_ref[rows_of(q, w), :] = (gate_grad * row_scale).astype(bf16)
        factors = []
        pending = []

        def beside():
            rate = jnp.sum(gate_grad * summed, axis=-1, keepdims=True)
            rate_out[pl.ds(q, w)] = jnp.broadcast_to(rate, (w * tok, 128)).reshape((w, tok, 128))
            rate_copy(q, w).start()

        def convert(k, total):
            if not factors:
                rate_copy(q, w).wait_recv()
                both = stacked(rate_out, q, w)[:, :1] + stacked(rate_in, q, w)[:, :1]
                factors.append(both * (row_scale * row_scale * row_scale) / (n * width))
            target = near[k]
            _, delta, united = mixed(q, w, target)
            mix = mix_ref[target]
            grad_united = total * gain_ref[target] - factors[0] * united
            moved = stacked(link_ref, q, w) * (grad_united * mix)
            below = grad_united * (1.0 - mix) + pltpu.roll(moved, w * tok - 1, 0)
            if k == 0:
                below = below + stacked(ag.at[1], q, w, me).astype(f32)
            pending.append((k, total * united, grad_united * delta))
            return below

        def send(group):
            @pl.when(sec > 0)
            def _():
                for j in range(w):
                    for k in group:
                        part_copy(1, q + j, away[k]).start()

            for k, gain_rows, mix_rows in pending:
                for j in range(w):
                    own = slice(j * tok, (j + 1) * tok)
                    p = lax.rem(q + j, 2)
                    vec_out[away[k], p] += jnp.sum(gain_rows[own], axis=0, keepdims=True)
                    vec_out[away[k], 2 + p] += jnp.sum(mix_rows[own], axis=0, keepdims=True)
            pending.clear()

            @pl.when(q + w == packs)
            def _():
                for k in group:
                    if k > 0:
                        vec_copy(away[k]).start()

        scatter(1, q, w, gate_ref, w_in, beside, convert, send)

    def runs(plan, enter, work):
        starts = [sum(c * w for c, w in plan[:i]) for i in range(len(plan))]
        for i, (count, w) in enumerate(plan):

            @pl.loop(0, count)
            def _(g, i=i, count=count, w=w):
                q = starts[i] + g * w

                def step():
                    if count > 1:

                        @pl.when(g < count - 1)
                        def _():
                            enter(q + w, w)

                    if i + 1 < len(plan):

                        @pl.when(g == count - 1)
                        def _():
                            enter(starts[i + 1], plan[i + 1][1])

                work(q, w, step)

    @pl.when(sec == last)
    def _():
        @pl.loop(0, packs)
        def _(q):
            enter_backward(q, 1)

        for j in range(n):
            load_out(j).wait()

        @pl.loop(0, packs)
        def _(q):
            backward(q, 1, lambda: None)

    def work_forward(q, w, step):
        forward(q, w, step)

        @pl.when(sec < last)
        def _():
            scatter_forward(q, w)

        @pl.when(sec == last)
        def _():
            scatter_backward(q, w)

    def work_backward(q, w, step):
        backward(q, w, step)
        scatter_backward(q, w)

    enter_forward(0, plans[0][0][1])
    runs(plans[0], enter_forward, work_forward)

    @pl.when(sec < last)
    def _():
        enter_backward(0, plans[1][0][1])
        runs(plans[1], enter_backward, work_backward)

    for phase in range(2):
        wait_bytes(ag.at[phase, :, pl.ds(0, n - 1)], ag_send.at[phase])
    wait_bytes(pair_out.at[1], pair_send.at[1])
    wait_bytes(rate_out, rate_send)

    @pl.when(sec < last)
    def _():
        wait_bytes(pair_out.at[0], pair_send.at[0])
        wait_bytes(part_out.at[0], rs_send.at[0])

    @pl.when(sec > 0)
    def _():
        wait_bytes(part_out.at[1], rs_send.at[1])

    sums = vec_out[chip]
    if chips > 1:
        wait_bytes(vec_in.at[pl.ds(0, chips - 1)], vec_recv)
        for k in range(1, chips):
            sums = sums + vec_in[away[k]]
        wait_bytes(vec_out.at[pl.ds(0, chips - 1)], vec_send)
    vec_sums[...] = sums


def grads_kernel(wide_ref, deep_ref, vec_ref, grad_in, grad_out, gain, mix):
    def summed(left, right):
        return lax.dot_general(left, right, TN, preferred_element_type=jnp.float32)

    def twice_rounded(acc):
        pair = [vec_ref[acc + p].astype(jnp.bfloat16).astype(jnp.float32) for p in range(2)]
        return pair[0] + pair[1]

    grad_in[0] = summed(deep_ref[0], wide_ref[0, 0]).astype(grad_in.dtype)
    grad_out[0] = summed(deep_ref[1], wide_ref[1, 0]).astype(grad_out.dtype)
    gain[...] = twice_rounded(0)
    mix[...] = twice_rounded(2)


def local(
    entering, output_grad, live_counts, segment_ids, weight_in, weight_out, norm_gain, shift_mix
):
    sections = lax.axis_size("section")
    n = lax.axis_size("tp")
    relays, micro, tok, width = entering.shape
    packs = relays * micro
    plans = (FORWARD, BACKWARD)
    hidden = weight_in.shape[2]
    width_all = weight_in.shape[1]
    chips = n // 2
    total = packs * tok
    bf16, f32 = jnp.bfloat16, jnp.float32
    vmem = pl.BlockSpec(memory_space=pltpu.VMEM)
    smem = pl.BlockSpec(memory_space=pltpu.SMEM)
    hbm = pl.BlockSpec(memory_space=pl.ANY)
    dma = pltpu.SemaphoreType.DMA
    wide, deep, vec_sums = pl.pallas_call(
        functools.partial(relay_kernel, n, sections, plans),
        out_shape=(
            jax.ShapeDtypeStruct((2, n, total, width), bf16),
            jax.ShapeDtypeStruct((2, total, hidden), bf16),
            jax.ShapeDtypeStruct((4, 1, width), f32),
        ),
        in_specs=[smem] + [vmem] * 5 + [hbm] * 2,
        out_specs=(vmem,) * 3,
        scratch_shapes=[
            pltpu.VMEM((2, packs, n, tok, width), bf16),
            pltpu.VMEM((2, packs, chips, tok, width), bf16),
            pltpu.VMEM((2, packs, chips, tok, width), bf16),
            pltpu.VMEM((2, packs, chips, tok, width), bf16),
            pltpu.VMEM((2, packs, chips, tok, width), bf16),
            pltpu.VMEM((packs, tok, 1), f32),
            pltpu.VMEM((packs, tok, 1), f32),
            pltpu.VMEM((n, 1, width), f32),
            pltpu.VMEM((n, 1, width), f32),
            pltpu.VMEM((n, hidden, width), bf16),
            pltpu.VMEM((n, hidden, width), bf16),
            pltpu.VMEM((total, hidden), f32),
            pltpu.VMEM((total, hidden), f32),
            pltpu.VMEM((total, hidden), f32),
            pltpu.VMEM((total, 128), f32),
            pltpu.VMEM((packs, tok, 128), f32),
            pltpu.VMEM((packs, tok, 128), f32),
            pltpu.VMEM((chips, 4, 1, width), f32),
            pltpu.VMEM((chips, 4, 1, width), f32),
            dma((2,)),
            dma((2, packs, n)),
            dma((2,)),
            dma((2, packs, chips)),
            dma((2,)),
            dma((2, packs)),
            dma,
            dma((packs,)),
            dma,
            dma,
            dma((2, n)),
        ],
        compiler_params=pltpu.CompilerParams(
            collective_id=0, has_side_effects=True, vmem_limit_bytes=44 * 1024 * 1024
        ),
        name="relays",
    )(
        live_counts,
        entering,
        output_grad,
        jnp.swapaxes(segment_ids, 0, 1),
        norm_gain,
        shift_mix,
        jnp.swapaxes(weight_in[0], 0, 1),
        weight_out[0],
    )

    part = pl.BlockSpec((2, 1, total, width), lambda j: (0, j, 0, 0))
    whole = pl.BlockSpec((2, total, hidden), lambda j: (0, 0, 0))
    sums = pl.BlockSpec((4, 1, width), lambda j: (0, 0, 0))
    row = pl.BlockSpec((1, width), lambda j: (0, 0))
    grad_in, grad_out, gain, mix = pl.pallas_call(
        grads_kernel,
        grid=(n,),
        out_shape=(
            jax.ShapeDtypeStruct((1, hidden, width_all), bf16),
            jax.ShapeDtypeStruct((1, hidden, width_all), bf16),
            jax.ShapeDtypeStruct((1, width), f32),
            jax.ShapeDtypeStruct((1, width), f32),
        ),
        in_specs=[part, whole, sums],
        out_specs=(
            pl.BlockSpec((1, hidden, width), lambda j: (0, 0, j)),
            pl.BlockSpec((1, hidden, width), lambda j: (0, 0, j)),
            row,
            row,
        ),
        compiler_params=pltpu.CompilerParams(
            dimension_semantics=("arbitrary",), vmem_limit_bytes=24 * 1024 * 1024
        ),
        name="weight_grads",
    )(wide, deep, vec_sums)
    return jnp.swapaxes(grad_in, 1, 2), grad_out, gain, mix


def solution(mesh):
    in_specs = (
        P(None, None, None, "tp"),
        P(None, None, None, "tp"),
        P(),
        P(),
        P("section", None, "tp"),
        P("section", "tp", None),
        P("section", None),
        P("section", None),
    )
    out_specs = (
        P("section", None, "tp"),
        P("section", "tp", None),
        P("section", "tp"),
        P("section", "tp"),
    )
    return jax.shard_map(local, mesh=mesh, in_specs=in_specs, out_specs=out_specs, check_vma=False)
```
